256 devices in a mesh: clients: 32 (over z_hi, y, core), fsdp: 8 (over x, z_lo).
Axes of the slice: x: 4, y: 4, z: 8 (z_hi: 4, z_lo: 2; z = z_hi * 2 + z_lo), core: 2. Of those that a mesh axis runs over, the one named last changes fastest.
Arguments:
- token_ids: int32 [32, 5120], P('clients', 'fsdp'), may hold values from 0 to 16383
- target: bfloat16 [32, 5120, 768], P('clients', 'fsdp'), may hold values from -6 to 6
- embedding: bfloat16 [16384, 768], P(None, 'fsdp'), may hold values from -6 to 6
- norm_gain: float32 [768], replicated, may hold values from 0.1 to 1.9
- global_model: float32 [3, 768, 1024], P(None, 'fsdp', 'clients'), may hold values from -0.21875 to 0.21875
- global_control: float32 [3, 768, 1024], P(None, 'fsdp', 'clients'), may hold values from -140 to 140
- client_control: float32 [32, 3, 768, 1024], P('clients', None, 'fsdp'), may hold values from -150 to 150
- local_steps: int32 [32], replicated, may hold values from 1 to 2
- client_weight: int32 [32], replicated, may hold values from 1 to 4
Outputs:
- server_step: float32 [3, 768, 1024], P(None, 'fsdp', 'clients')
- server_control: float32 [3, 768, 1024], P(None, 'fsdp', 'clients')
- client_update: float32 [32, 3, 768, 1024], P('clients', None, 'fsdp')
The draws below stay inside these ranges and needn't reach their ends.
All inputs are finite; a program needn't handle non-finite values.
Results may differ from the reference program's by a relative error of at most 0.025.
Values may be sent and summed in bfloat16 or wider, within the bound.
No kernel may reach another device: no remote copies, remote signals or barrier semaphores. Data moves between devices by JAX's collectives and lax.ppermute only.
A program may use at most 64 MiB of HBM per device.

```python
import math
import jax
import jax.numpy as jnp
import numpy as np
from jax import lax

D = 768
FF = 1024
VOCAB = 16384
LOCAL = 2
TOK_DEV = 640
GROUP_TOK = 5120
CLIENTS = 32
N_FSDP = 8


def control_common(key):
    row_key, col_key, jitter_key = jax.random.split(jax.random.fold_in(key, 7001), 3)
    lowest = 0.5
    highest = 2.0
    jitter = jax.random.truncated_normal(jitter_key, -4.0, 4.0, (3, D, FF), jnp.float32)
    row_scale = jnp.exp(jax.random.uniform(row_key, (1, D, 1), jnp.float32, math.log(lowest), math.log(highest)))
    col_scale = jnp.exp(jax.random.uniform(col_key, (1, 1, FF), jnp.float32, math.log(lowest), math.log(highest)))
    return 5.0 * row_scale * col_scale * jitter


def draw_global_control(key, part):
    return control_common(key)


def draw_client_control(key, part):
    common = control_common(key)
    drift_key, pair_key = jax.random.split(jax.random.fold_in(key, 7002), 2)
    drifts = 0.5 * jax.random.truncated_normal(drift_key, -4.0, 4.0, (CLIENTS, 3, D, FF), jnp.float32)
    pairing = jax.random.permutation(pair_key, CLIENTS)
    span_width = FF // CLIENTS
    owners = jnp.arange(FF) // span_width
    spike_factor = jnp.where(owners[None, :] == pairing[:, None], 4.0, 1.0).astype(jnp.float32)
    return common[None] + drifts * spike_factor[:, None, None, :]


def place_ends(values, own_key, low, largest):
    longest = values.shape.index(max(values.shape))
    spots = []
    for shift in (0, 1):
        where = [jax.random.randint(jax.random.fold_in(own_key, axis), (), 0, length) for axis, length in enumerate(values.shape)]
        where[longest] = (where[longest] + shift) % values.shape[longest]
        spots.append(tuple(where))
    return values.at[spots[0]].set(low).at[spots[1]].set(largest)


def block_scale(own_key, dims, shards, least, high):
    gain, own = 1.0, jax.random.fold_in(own_key, 6)
    for position, shards_of in shards:
        heights = jnp.exp(jax.random.uniform(jax.random.fold_in(own, position), (shards_of,), jnp.float32, least / len(shards), high / len(shards)))
        gain = gain * jnp.repeat(heights, dims[position] // shards_of).reshape([-1 if axis == position else 1 for axis in range(len(dims))])
    return gain


def rank_bounds(amount, slope):
    loads = [(1 << 20) // math.isqrt(standing ** slope) + 1 for standing in range(1, amount + 1)]
    spread = 1 + sum(loads) // (1 << 30)
    return np.cumsum(np.array([max(1, weight // spread) for weight in loads]))


def ranked_ids(stream_key, dims, number_of, lean):
    grid = rank_bounds(number_of, lean)
    lot = jax.random.randint(jax.random.fold_in(stream_key, 1), dims, 0, int(grid[number_of - 1]))
    grade = jnp.searchsorted(jnp.asarray(grid, jnp.int32), lot, side="right")
    return jax.random.permutation(jax.random.fold_in(stream_key, 2), number_of)[grade].astype(jnp.int32)


def centred(rng, dims, spread, reach, cuts=(), held_as=jnp.bfloat16):
    array = spread * jax.random.normal(rng, dims, jnp.float32)
    if cuts:
        array = array * block_scale(rng, dims, cuts, -0.22, 0.18)
    return jnp.clip(array, -reach, reach).astype(held_as)


def setup_inputs(seed: int = 0) -> dict:
    arg_keys = jax.random.split(jax.random.key(seed), 10)
    token_ids = place_ends(ranked_ids(arg_keys[0], (CLIENTS, GROUP_TOK), VOCAB, 2), jax.random.fold_in(arg_keys[0], 3), 0, VOCAB - 1).astype(jnp.int32)
    target = centred(arg_keys[1], (CLIENTS, GROUP_TOK, D), 1.0, 6.0, ((0, 32), (1, 8)))
    embedding = centred(arg_keys[2], (VOCAB, D), 1.0, 6.0, ((1, 8),))
    norm_gain = jnp.clip(1.0 + 0.18 * jax.random.normal(arg_keys[3], (D,), jnp.float32), 0.1, 1.9)
    global_model = centred(arg_keys[4], (3, D, FF), D ** -0.5, 0.21875, ((1, 8), (2, 32)), jnp.float32)
    global_control = draw_global_control(jax.random.fold_in(arg_keys[9], 71), 0)
    client_control = draw_client_control(jax.random.fold_in(arg_keys[9], 71), 0)
    local_steps = place_ends(jax.random.randint(arg_keys[7], (CLIENTS,), 1, LOCAL + 1), jax.random.fold_in(arg_keys[7], 1), 1, LOCAL).astype(jnp.int32)
    client_weight = place_ends(jax.random.randint(arg_keys[8], (CLIENTS,), 1, 5), jax.random.fold_in(arg_keys[8], 1), 1, 4).astype(jnp.int32)
    return {"token_ids": token_ids, "target": target, "embedding": embedding, "norm_gain": norm_gain, "global_model": global_model, "global_control": global_control, "client_control": client_control, "local_steps": local_steps, "client_weight": client_weight}


learning_rate = 0.005
norm_eps = 1e-06

def gelu_pair(pre_act):
    return jax.vjp(lambda inputs: jax.nn.gelu(inputs, approximate=True), pre_act)

def shard_grads(normed, embedded, target, current, loss_scale):
    gate_pre = jnp.dot(normed, current[0], preferred_element_type=jnp.float32)
    up_pre = jnp.dot(normed, current[1], preferred_element_type=jnp.float32)
    gate_act, gelu_back = gelu_pair(gate_pre)
    hidden = (gate_act * up_pre).astype(jnp.bfloat16)
    projected = lax.dot_general(hidden, current[2], (((1,), (1,)), ((), ())), preferred_element_type=jnp.float32)
    out_grad = ((embedded.astype(jnp.float32) + projected - target.astype(jnp.float32)) * loss_scale).astype(jnp.bfloat16)
    grad_outer = lax.dot_general(out_grad, hidden, (((0,), (0,)), ((), ())), preferred_element_type=jnp.float32)
    hidden_grad = jnp.dot(out_grad, current[2], preferred_element_type=jnp.float32)
    gate_grad = gelu_back(hidden_grad * up_pre)[0].astype(jnp.bfloat16)
    up_grad = (hidden_grad * gate_act).astype(jnp.bfloat16)
    grad_gate = lax.dot_general(normed, gate_grad, (((0,), (0,)), ((), ())), preferred_element_type=jnp.float32)
    grad_up = lax.dot_general(normed, up_grad, (((0,), (0,)), ((), ())), preferred_element_type=jnp.float32)
    return jnp.stack([grad_gate, grad_up, grad_outer])

def client_round(inputs, embedding, norm_gain, global_model, global_control):
    ids_row, target_rows, own_control, step_count = inputs
    embedded = jnp.take(embedding, ids_row, axis=0)
    widened = embedded.astype(jnp.float32)
    inv_norm = lax.rsqrt(lax.optimization_barrier(jnp.mean(widened * widened, axis=1, keepdims=True)) + norm_eps)
    normed = (widened * inv_norm * norm_gain).astype(jnp.bfloat16)
    loss_scale = 1.0 / math.sqrt(TOK_DEV * N_FSDP)
    shard_normed = normed.reshape(N_FSDP, TOK_DEV, -1)
    shard_embedded = embedded.reshape(N_FSDP, TOK_DEV, -1)
    shard_target = target_rows.reshape(N_FSDP, TOK_DEV, -1)
    correction = global_control - own_control
    pseudo = jnp.zeros(global_model.shape, jnp.float32)
    for local_step in range(LOCAL):
        current = (global_model - learning_rate * pseudo).astype(jnp.bfloat16)

        def add_shard(running, pieces):
            term = shard_grads(pieces[0], pieces[1], pieces[2], current, loss_scale)
            rounded = lax.optimization_barrier(term.astype(jnp.bfloat16))
            return (running + rounded.astype(jnp.float32), None)
        grads, _ = lax.scan(add_shard, jnp.zeros(global_model.shape, jnp.float32), (shard_normed, shard_embedded, shard_target))
        step_mask = (local_step < step_count).astype(jnp.float32)
        pseudo = pseudo + step_mask * (grads + correction)
    update = own_control - global_control + pseudo / step_count.astype(jnp.float32)
    return (pseudo, update)

def reference(token_ids, target, embedding, norm_gain, global_model, global_control, client_control, local_steps, client_weight):

    def one_client(inputs):
        return client_round(inputs, embedding, norm_gain, global_model, global_control)
    pseudo_all, client_update = lax.map(one_client, (token_ids, target, client_control, local_steps))
    weights = client_weight.astype(jnp.float32)
    weight_total = jnp.sum(weights)
    server_step = lax.optimization_barrier(jnp.sum(weights[:, None, None, None] * pseudo_all, axis=0)) / weight_total
    server_control = lax.optimization_barrier(jnp.sum(weights[:, None, None, None] * client_update, axis=0)) / weight_total
    return (server_step, server_control, client_update)
```

```python
import math

import jax
import jax.numpy as jnp
from jax import lax
from jax.sharding import PartitionSpec as P

LOCAL = 2


learning_rate = 0.005
norm_eps = 1e-06


def peer(place, offset, size):
    x_size = size // 2
    return ((place // 2 + offset // 2) % x_size) * 2 + ((place % 2) ^ (offset % 2))


def opposite(offset, size):
    return ((-(offset // 2)) % (size // 2)) * 2 + offset % 2


def shifted(x, offset):
    size = lax.axis_size("fsdp")
    return lax.ppermute(x, "fsdp", [(i, peer(i, offset, size)) for i in range(size)])


def far_first(size):
    x_size = size // 2
    return [2 * dx for dx in sorted(range(1, x_size), key=lambda dx: -min(dx, x_size - dx))]


def swapped_cores(x):
    return lax.ppermute(x, "clients", [(i, i ^ 1) for i in range(lax.axis_size("clients"))])


def spread(blocks):
    size = len(blocks)
    arrived = [blocks[0]] + [None] * (size - 1)
    for j in far_first(size):
        for offset in (j + 1, j):
            arrived[opposite(offset, size)] = shifted(blocks[offset], offset)
    arrived[1] = shifted(blocks[1], 1)
    return arrived


def gathered(block, size):
    partner = shifted(block, 1)
    arrived = [block, partner] + [None] * (size - 2)
    for base, own in ((0, block), (1, partner)):
        for j in far_first(size):
            arrived[opposite(j, size) + base] = shifted(own, j)
    return arrived


def summed(blocks):
    size = len(blocks)
    for_partner, for_me = blocks[1].astype(jnp.float32), blocks[0].astype(jnp.float32)
    came = [shifted(blocks[j + 1], j) for j in far_first(size)]
    mine = [shifted(blocks[j], j) for j in far_first(size)]
    for block in came:
        for_partner += block.astype(jnp.float32)
    partner = shifted(for_partner.astype(jnp.bfloat16), 1)
    for block in mine:
        for_me += block.astype(jnp.float32)
    return for_me + partner.astype(jnp.float32)


def same_core_groups():
    size = lax.axis_size("clients")
    return [[2 * k + core for k in range(size // 2)] for core in range(2)]


def turned(x, contract):
    eye = jnp.eye(x.shape[contract], dtype=x.dtype)
    dims = (((1,), (1,)), ((), ())) if contract else (((0,), (0,)), ((), ()))
    both = (eye, x) if contract else (x, eye)
    return lax.dot_general(*both, dims, preferred_element_type=jnp.float32).astype(x.dtype)


def gather_clients(x):
    a, rows, cols = x.shape
    groups = same_core_groups()
    count = len(groups[0])
    block = jnp.swapaxes(x, 1, 2).reshape(a * cols, rows)
    mine = lax.all_to_all(
        jnp.broadcast_to(block[None], (count, *block.shape)),
        "clients",
        0,
        0,
        tiled=True,
        axis_index_groups=groups,
    )
    theirs = swapped_cores(mine)
    first = lax.axis_index("clients") % 2 == 0
    both = jnp.stack([jnp.where(first, mine, theirs), jnp.where(first, theirs, mine)], axis=1)
    both = both.reshape(count, 2, a, cols, rows)
    return [turned(both[:, :, k].reshape(count * 2 * cols, rows), 1) for k in range(a)]


def sum_clients(arrays):
    rows, cols = arrays[0].shape
    a = len(arrays)
    groups = same_core_groups()
    count = len(groups[0])
    part = cols // (2 * count)
    cut = jnp.stack([turned(x, 0).reshape(count, 2, part, rows) for x in arrays], axis=2)
    cut = cut.reshape(count, 2, a * part, rows)
    core = lax.axis_index("clients") % 2
    kept = lax.dynamic_index_in_dim(cut, core, 1, keepdims=False)
    given = lax.dynamic_index_in_dim(cut, 1 - core, 1, keepdims=False)
    came = swapped_cores(given)
    pair = (kept.astype(jnp.float32) + came.astype(jnp.float32)).astype(jnp.bfloat16)
    arrived = lax.all_to_all(pair, "clients", 0, 0, tiled=True, axis_index_groups=groups)
    total = arrived.astype(jnp.float32).sum(axis=0)
    return jnp.swapaxes(total.reshape(a, part, rows), 1, 2)


def gelu_pair(pre_act):
    return jax.vjp(lambda inputs: jax.nn.gelu(inputs, approximate=True), pre_act)


def contract_rows(left, right):
    return lax.dot_general(
        left, right, (((0,), (0,)), ((), ())), preferred_element_type=jnp.float32
    )


def local_grads(normed, residual, weights, loss_scale):
    gate_w, up_w, out_w = weights
    gate_pre = jnp.dot(normed, gate_w, preferred_element_type=jnp.float32)
    up_pre = jnp.dot(normed, up_w, preferred_element_type=jnp.float32)
    gate_act, gelu_back = gelu_pair(gate_pre)
    hidden = (gate_act * up_pre).astype(jnp.bfloat16)
    projected = lax.dot_general(
        hidden, out_w, (((1,), (1,)), ((), ())), preferred_element_type=jnp.float32
    )
    out_grad = ((residual + projected) * loss_scale).astype(jnp.bfloat16)
    hidden_grad = jnp.dot(out_grad, out_w, preferred_element_type=jnp.float32)
    gate_grad = gelu_back(hidden_grad * up_pre)[0].astype(jnp.bfloat16)
    up_grad = (hidden_grad * gate_act).astype(jnp.bfloat16)
    return [
        contract_rows(normed, gate_grad).astype(jnp.bfloat16),
        contract_rows(normed, up_grad).astype(jnp.bfloat16),
        contract_rows(out_grad, hidden).astype(jnp.bfloat16),
    ]


def summed_terms(terms, size):
    rows = terms[0].shape[0] // size
    return summed(
        [jnp.concatenate([t[j * rows : (j + 1) * rows] for t in terms]) for j in range(size)]
    )


def joined(pieces, count):
    rows = pieces[0].shape[0] // count
    return [
        jnp.concatenate([p[k * rows : (k + 1) * rows] for p in pieces]) for k in range(count)
    ]


def body(
    token_ids,
    target,
    embedding,
    norm_gain,
    global_model,
    global_control,
    client_control,
    local_steps,
    client_weight,
):
    size = lax.axis_size("fsdp")
    place = lax.axis_index("fsdp")
    core = lax.axis_index("clients") % 2
    width = embedding.shape[1]
    tok_rows = target.shape[1]
    loss_scale = 1.0 / math.sqrt(tok_rows * size)

    all_ids = lax.all_to_all(
        jnp.broadcast_to(token_ids, (size, tok_rows)), "fsdp", 0, 0, tiled=True
    )
    looked_up = [
        embedding.at[lax.dynamic_index_in_dim(all_ids, peer(place, j, size), 0, False)].get(
            mode="promise_in_bounds"
        )
        for j in range(size)
    ]
    embedded = jnp.concatenate(spread(looked_up), axis=1)
    widened = embedded.astype(jnp.float32)
    order = jnp.stack([peer(place, j, size) for j in range(size)])
    gain = jnp.take(norm_gain.reshape(size, width), order, axis=0).reshape(-1)
    inv_norm = lax.rsqrt(jnp.mean(widened * widened, axis=1, keepdims=True) + norm_eps)
    normed = (widened * inv_norm * gain).astype(jnp.bfloat16)
    wanted = (order[:, None] * width + jnp.arange(width)[None, :]).reshape(-1)
    reorder = (jnp.arange(size * width)[:, None] == wanted[None, :]).astype(jnp.bfloat16)
    residual = widened - jnp.dot(target[0], reorder, preferred_element_type=jnp.float32)

    model_rows = jnp.concatenate(gather_clients(global_model.astype(jnp.bfloat16)))
    half = model_rows.shape[1] // 2
    half_rows = lax.dynamic_slice_in_dim(model_rows, core * half, half, axis=1)
    half_all = jnp.stack(joined(gathered(half_rows, size), 3))
    weights = jnp.concatenate([half_all, swapped_cores(half_all)], axis=2)

    control_rows = jnp.concatenate(gather_clients(global_control.astype(jnp.bfloat16)))
    client_index = lax.axis_index("clients")
    slots = jnp.arange(local_steps.shape[0])
    step_count = jnp.sum(jnp.where(slots == client_index, local_steps, 0)).astype(jnp.float32)
    own_weight = jnp.sum(jnp.where(slots == client_index, client_weight, 0)).astype(jnp.float32)
    weight_total = jnp.sum(client_weight).astype(jnp.float32)
    second = (step_count > 1.5).astype(jnp.float32)
    own_control = client_control[0].reshape(control_rows.shape)
    correction = control_rows.astype(jnp.float32) - own_control

    grads = summed_terms(local_grads(normed, residual, weights, loss_scale), size)
    grads = jnp.where(
        core == 0, grads, jnp.concatenate([grads[:, half:], grads[:, :half]], axis=1)
    )
    current = (
        model_rows.astype(jnp.float32) - learning_rate * (grads + correction)
    ).astype(jnp.bfloat16)
    weights = joined(gathered(current, size), 3)

    early = sum_clients(
        jnp.split((own_weight * (grads + step_count * correction)).astype(jnp.bfloat16), 3)
        + jnp.split((own_weight / step_count * grads).astype(jnp.bfloat16), 3)
    )
    last = second * summed_terms(local_grads(normed, residual, weights, loss_scale), size)
    late = sum_clients(jnp.split((own_weight * last).astype(jnp.bfloat16), 3))
    update = ((grads + last) / step_count).reshape(client_control.shape)
    steps_total = jnp.sum(local_steps * client_weight).astype(jnp.float32)
    rounded_away = global_control - global_control.astype(jnp.bfloat16).astype(jnp.float32)
    server_step = (early[:3] + late + steps_total * rounded_away) / weight_total
    server_control = (early[3:] + 0.5 * late) / weight_total
    return (server_step, server_control, update)


def solution(mesh):
    placed = (
        P("clients", "fsdp"),
        P("clients", "fsdp", None),
        P(None, "fsdp"),
        P(),
        P(None, "fsdp", "clients"),
        P(None, "fsdp", "clients"),
        P("clients", None, "fsdp", None),
        P(),
        P(),
    )
    return jax.shard_map(
        body,
        mesh=mesh,
        in_specs=placed,
        out_specs=(
            P(None, "fsdp", "clients"),
            P(None, "fsdp", "clients"),
            P("clients", None, "fsdp", None),
        ),
        check_vma=False,
    )
```

```python
import math

import jax
import jax.numpy as jnp
from jax import lax
from jax.sharding import PartitionSpec as P

LOCAL = 2


learning_rate = 0.005
norm_eps = 1e-06


BOTH = ("clients", "fsdp")


def moved(block, dx, dz=0):
    clients, size = lax.axis_size("clients"), lax.axis_size("fsdp")
    pairs = []
    for client in range(clients):
        for place in range(size):
            x = (place // 2 + dx) % (size // 2)
            z, core = (place % 2) ^ dz, client % 2
            target = (client - core + z) * size + 2 * x + core
            pairs.append((client * size + place, target))
    return lax.ppermute(block, BOTH, pairs)


def peer(place, offset, size):
    x_size = size // 2
    return ((place // 2 + offset // 2) % x_size) * 2 + ((place % 2) ^ (offset % 2))


def far_first(size):
    x_size = size // 2
    return sorted(range(x_size), key=lambda dx: -min(dx, x_size - dx))


def swapped_cores(x):
    return lax.ppermute(x, "clients", [(i, i ^ 1) for i in range(lax.axis_size("clients"))])


def gathered(block, size):
    x_size = size // 2
    arrived = [None] * size
    for dx in far_first(size):
        back = 2 * (-dx % x_size)
        arrived[back] = moved(block, dx)
    for dx in far_first(size):
        back = 2 * (-dx % x_size)
        arrived[back + 1] = swapped_cores(arrived[back])
    return arrived


def summed(blocks):
    size = len(blocks)
    pairs = [
        (
            blocks[2 * dx].astype(jnp.float32)
            + swapped_cores(blocks[2 * dx + 1]).astype(jnp.float32)
        ).astype(jnp.bfloat16)
        for dx in range(size // 2)
    ]
    arrived = [moved(pairs[dx], dx) for dx in far_first(size)]
    return sum(a.astype(jnp.float32) for a in arrived)


def same_core_groups():
    size = lax.axis_size("clients")
    return [[2 * k + core for k in range(size // 2)] for core in range(2)]


def turned(x, contract):
    eye = jnp.eye(x.shape[contract], dtype=x.dtype)
    dims = (((1,), (1,)), ((), ())) if contract else (((0,), (0,)), ((), ()))
    both = (eye, x) if contract else (x, eye)
    return lax.dot_general(*both, dims, preferred_element_type=jnp.float32).astype(x.dtype)


def gather_clients(x):
    a, rows, cols = x.shape
    groups = same_core_groups()
    count = len(groups[0])
    block = jnp.swapaxes(x, 1, 2).reshape(a * cols, rows)
    mine = lax.all_to_all(
        jnp.broadcast_to(block[None], (count, *block.shape)),
        "clients",
        0,
        0,
        tiled=True,
        axis_index_groups=groups,
    )
    theirs = swapped_cores(mine)
    first = lax.axis_index("clients") % 2 == 0
    both = jnp.stack([jnp.where(first, mine, theirs), jnp.where(first, theirs, mine)], axis=1)
    both = both.reshape(count, 2, a, cols, rows)
    return [turned(both[:, :, k].reshape(count * 2 * cols, rows), 1) for k in range(a)]


def sum_clients(arrays):
    rows, cols = arrays[0].shape
    a = len(arrays)
    groups = same_core_groups()
    count = len(groups[0])
    part = cols // (2 * count)
    cut = jnp.stack([turned(x, 0).reshape(count, 2, part, rows) for x in arrays], axis=2)
    cut = cut.reshape(count, 2, a * part, rows)
    core = lax.axis_index("clients") % 2
    kept = lax.dynamic_index_in_dim(cut, core, 1, keepdims=False)
    given = lax.dynamic_index_in_dim(cut, 1 - core, 1, keepdims=False)
    came = swapped_cores(given)
    pair = (kept.astype(jnp.float32) + came.astype(jnp.float32)).astype(jnp.bfloat16)
    arrived = lax.all_to_all(pair, "clients", 0, 0, tiled=True, axis_index_groups=groups)
    total = arrived.astype(jnp.float32).sum(axis=0)
    return jnp.swapaxes(total.reshape(a, part, rows), 1, 2)


def gelu_pair(pre_act):
    return jax.vjp(lambda inputs: jax.nn.gelu(inputs, approximate=True), pre_act)


def contract_rows(left, right):
    return lax.dot_general(
        left, right, (((0,), (0,)), ((), ())), preferred_element_type=jnp.float32
    )


def local_grads(normed, residual, weights, loss_scale):
    gate_w, up_w, out_w = weights
    gate_pre = jnp.dot(normed, gate_w, preferred_element_type=jnp.float32)
    up_pre = jnp.dot(normed, up_w, preferred_element_type=jnp.float32)
    gate_act, gelu_back = gelu_pair(gate_pre)
    hidden = (gate_act * up_pre).astype(jnp.bfloat16)
    projected = lax.dot_general(
        hidden, out_w, (((1,), (1,)), ((), ())), preferred_element_type=jnp.float32
    )
    out_grad = ((residual + projected) * loss_scale).astype(jnp.bfloat16)
    hidden_grad = jnp.dot(out_grad, out_w, preferred_element_type=jnp.float32)
    gate_grad = gelu_back(hidden_grad * up_pre)[0].astype(jnp.bfloat16)
    up_grad = (hidden_grad * gate_act).astype(jnp.bfloat16)
    return [
        contract_rows(normed, gate_grad).astype(jnp.bfloat16),
        contract_rows(normed, up_grad).astype(jnp.bfloat16),
        contract_rows(out_grad, hidden).astype(jnp.bfloat16),
    ]


def summed_terms(terms, size):
    rows = terms[0].shape[0] // size
    return summed(
        [jnp.concatenate([t[j * rows : (j + 1) * rows] for t in terms]) for j in range(size)]
    )


def joined(pieces, count):
    rows = pieces[0].shape[0] // count
    return [
        jnp.concatenate([p[k * rows : (k + 1) * rows] for p in pieces]) for k in range(count)
    ]


def body(
    token_ids,
    target,
    embedding,
    norm_gain,
    global_model,
    global_control,
    client_control,
    local_steps,
    client_weight,
):
    size = lax.axis_size("fsdp")
    place = lax.axis_index("fsdp")
    core = lax.axis_index("clients") % 2
    width = embedding.shape[1]
    tok_rows = target.shape[1]
    loss_scale = 1.0 / math.sqrt(tok_rows * size)

    all_ids = lax.all_to_all(
        jnp.broadcast_to(token_ids, (size, tok_rows)), "fsdp", 0, 0, tiled=True
    )
    model_rows = jnp.concatenate(gather_clients(global_model.astype(jnp.bfloat16)))
    looked_up = embedding.at[all_ids.reshape(-1)].get(mode="promise_in_bounds")

    worker_place = place - place % 2 + core
    order = jnp.stack([peer(worker_place, j, size) for j in range(size)])
    wanted = (order[:, None] * width + jnp.arange(width)[None, :]).reshape(-1)
    reorder = (jnp.arange(size * width)[:, None] == wanted[None, :]).astype(jnp.bfloat16)
    goal = jnp.dot(moved(target[0], 0), reorder, preferred_element_type=jnp.float32)
    goal = lax.optimization_barrier(goal.astype(jnp.bfloat16))
    gain = jnp.dot(
        norm_gain[None], reorder.astype(jnp.float32), precision=lax.Precision.HIGHEST
    )

    pieces = [None] * size
    for dx in far_first(size):
        for dz in (1, 0):
            rows = lax.dynamic_slice_in_dim(
                looked_up, peer(place, 2 * dx + dz, size) * tok_rows, tok_rows
            )
            pieces[2 * (-dx % (size // 2)) + dz] = moved(rows, dx, dz)
    stacked = lax.optimization_barrier(jnp.stack(pieces))
    embedded = jnp.moveaxis(stacked, 0, 1).reshape(tok_rows, size * width)
    widened = embedded.astype(jnp.float32)
    inv_norm = lax.rsqrt(jnp.mean(widened * widened, axis=1, keepdims=True) + norm_eps)
    normed = (widened * inv_norm * gain).astype(jnp.bfloat16)
    residual = widened - goal.astype(jnp.float32)

    weights = joined(gathered(model_rows, size), 3)

    late_control, _ = lax.optimization_barrier((global_control.astype(jnp.bfloat16), model_rows))
    control_rows = jnp.concatenate(gather_clients(late_control))
    client_index = lax.axis_index("clients")
    slots = jnp.arange(local_steps.shape[0])
    step_count = jnp.sum(jnp.where(slots == client_index, local_steps, 0)).astype(jnp.float32)
    own_weight = jnp.sum(jnp.where(slots == client_index, client_weight, 0)).astype(jnp.float32)
    weight_total = jnp.sum(client_weight).astype(jnp.float32)
    second = (step_count > 1.5).astype(jnp.float32)
    own_control = client_control[0].reshape(control_rows.shape)
    correction = control_rows.astype(jnp.float32) - own_control

    grads = summed_terms(local_grads(normed, residual, weights, loss_scale), size)
    current = (
        model_rows.astype(jnp.float32) - learning_rate * (grads + correction)
    ).astype(jnp.bfloat16)
    weights = joined(gathered(current, size), 3)

    early = sum_clients(
        jnp.split((own_weight * (grads + step_count * correction)).astype(jnp.bfloat16), 3)
        + jnp.split((own_weight / step_count * grads).astype(jnp.bfloat16), 3)
    )
    terms = local_grads(normed, residual, weights, loss_scale)
    terms, early = lax.optimization_barrier((terms, early))
    last = second * summed_terms(terms, size)
    late = sum_clients(jnp.split((own_weight * last).astype(jnp.bfloat16), 3))
    update = ((grads + last) / step_count).reshape(client_control.shape)
    steps_total = jnp.sum(local_steps * client_weight).astype(jnp.float32)
    rounded_away = global_control - global_control.astype(jnp.bfloat16).astype(jnp.float32)
    server_step = (early[:3] + late + steps_total * rounded_away) / weight_total
    server_control = (early[3:] + 0.5 * late) / weight_total
    return (server_step, server_control, update)


def solution(mesh):
    placed = (
        P("clients", "fsdp"),
        P("clients", "fsdp", None),
        P(None, "fsdp"),
        P(),
        P(None, "fsdp", "clients"),
        P(None, "fsdp", "clients"),
        P("clients", None, "fsdp", None),
        P(),
        P(),
    )
    return jax.shard_map(
        body,
        mesh=mesh,
        in_specs=placed,
        out_specs=(
            P(None, "fsdp", "clients"),
            P(None, "fsdp", "clients"),
            P("clients", None, "fsdp", None),
        ),
        check_vma=False,
    )
```

```python
import math

import jax
import jax.numpy as jnp
from jax import lax
from jax.sharding import PartitionSpec as P

LOCAL = 2


learning_rate = 0.005
norm_eps = 1e-06


BOTH = ("clients", "fsdp")


def moved(block, dx):
    clients, size = lax.axis_size("clients"), lax.axis_size("fsdp")
    pairs = []
    for client in range(clients):
        for place in range(size):
            x = (place // 2 + dx) % (size // 2)
            z, core = place % 2, client % 2
            target = (client - core + z) * size + 2 * x + core
            pairs.append((client * size + place, target))
    return lax.ppermute(block, BOTH, pairs)


def peer(place, offset, size):
    x_size = size // 2
    return ((place // 2 + offset // 2) % x_size) * 2 + ((place % 2) ^ (offset % 2))


def near_first(size):
    x_size = size // 2
    return sorted(range(x_size), key=lambda dx: min(dx, x_size - dx))


def swapped_cores(x):
    return lax.ppermute(x, "clients", [(i, i ^ 1) for i in range(lax.axis_size("clients"))])


def gathered(block, size):
    x_size = size // 2
    arrived = [None] * size
    for dx in near_first(size):
        back = 2 * (-dx % x_size)
        arrived[back] = moved(block, dx)
    for dx in near_first(size):
        back = 2 * (-dx % x_size)
        arrived[back + 1] = swapped_cores(arrived[back])
    return arrived


def summed(blocks):
    size = len(blocks)
    pairs = [
        (
            blocks[2 * dx].astype(jnp.float32)
            + swapped_cores(blocks[2 * dx + 1]).astype(jnp.float32)
        ).astype(jnp.bfloat16)
        for dx in range(size // 2)
    ]
    arrived = [moved(pairs[dx], dx) for dx in near_first(size)]
    return sum(a.astype(jnp.float32) for a in arrived)


def same_core_groups():
    size = lax.axis_size("clients")
    return [[2 * k + core for k in range(size // 2)] for core in range(2)]


def turned(x, contract):
    eye = jnp.eye(x.shape[contract], dtype=x.dtype)
    dims = (((1,), (1,)), ((), ())) if contract else (((0,), (0,)), ((), ()))
    both = (eye, x) if contract else (x, eye)
    return lax.dot_general(*both, dims, preferred_element_type=jnp.float32).astype(x.dtype)


def gather_clients(x):
    a, rows, cols = x.shape
    groups = same_core_groups()
    count = len(groups[0])
    block = jnp.swapaxes(x, 1, 2).reshape(a * cols, rows)
    mine = lax.all_to_all(
        jnp.broadcast_to(block[None], (count, *block.shape)),
        "clients",
        0,
        0,
        tiled=True,
        axis_index_groups=groups,
    )
    theirs = swapped_cores(mine)
    first = lax.axis_index("clients") % 2 == 0
    both = jnp.stack([jnp.where(first, mine, theirs), jnp.where(first, theirs, mine)], axis=1)
    both = both.reshape(count, 2, a, cols, rows)
    return [both[:, :, k].reshape(count * 2 * cols, rows) for k in range(a)]


def cut_for_clients(array, count):
    rows, cols = array.shape
    return turned(array, 0).reshape(count, 2, cols // (2 * count), rows)


def sum_clients(cuts):
    count, _, part, rows = cuts[0].shape
    a = len(cuts)
    cut = jnp.stack(cuts, axis=2).reshape(count, 2, a * part, rows)
    core = lax.axis_index("clients") % 2
    kept = lax.dynamic_index_in_dim(cut, core, 1, keepdims=False)
    given = lax.dynamic_index_in_dim(cut, 1 - core, 1, keepdims=False)
    came = swapped_cores(given)
    pair = (kept.astype(jnp.float32) + came.astype(jnp.float32)).astype(jnp.bfloat16)
    arrived = lax.all_to_all(
        pair, "clients", 0, 0, tiled=True, axis_index_groups=same_core_groups()
    )
    total = arrived.astype(jnp.float32).sum(axis=0)
    return jnp.swapaxes(total.reshape(a, part, rows), 1, 2)


def gelu_pair(pre_act):
    return jax.vjp(lambda inputs: jax.nn.gelu(inputs, approximate=True), pre_act)


def contract_rows(left, right):
    return lax.dot_general(
        left, right, (((0,), (0,)), ((), ())), preferred_element_type=jnp.float32
    )


def local_grads(normed, residual, weights, loss_scale):
    gate_w, up_w, out_w = weights
    gate_pre = jnp.dot(normed, gate_w, preferred_element_type=jnp.float32)
    up_pre = jnp.dot(normed, up_w, preferred_element_type=jnp.float32)
    gate_act, gelu_back = gelu_pair(gate_pre)
    hidden = (gate_act * up_pre).astype(jnp.bfloat16)
    projected = lax.dot_general(
        hidden, out_w, (((1,), (1,)), ((), ())), preferred_element_type=jnp.float32
    )
    out_grad = ((residual + projected) * loss_scale).astype(jnp.bfloat16)
    hidden_grad = jnp.dot(out_grad, out_w, preferred_element_type=jnp.float32)
    gate_grad = gelu_back(hidden_grad * up_pre)[0].astype(jnp.bfloat16)
    up_grad = (hidden_grad * gate_act).astype(jnp.bfloat16)
    return [
        contract_rows(normed, gate_grad).astype(jnp.bfloat16),
        contract_rows(normed, up_grad).astype(jnp.bfloat16),
        contract_rows(out_grad, hidden).astype(jnp.bfloat16),
    ]


def summed_terms(terms, size):
    rows = terms[0].shape[0] // size
    return summed(
        [jnp.concatenate([t[j * rows : (j + 1) * rows] for t in terms]) for j in range(size)]
    )


def joined(pieces, count):
    rows = pieces[0].shape[0] // count
    return [
        jnp.concatenate([p[k * rows : (k + 1) * rows] for p in pieces]) for k in range(count)
    ]


def body(
    token_ids,
    target,
    embedding,
    norm_gain,
    global_model,
    global_control,
    client_control,
    local_steps,
    client_weight,
):
    size = lax.axis_size("fsdp")
    place = lax.axis_index("fsdp")
    core = lax.axis_index("clients") % 2
    width = embedding.shape[1]
    tok_rows = target.shape[1]
    loss_scale = 1.0 / math.sqrt(tok_rows * size)

    server = gather_clients(
        jnp.concatenate([global_model, global_control]).astype(jnp.bfloat16)
    )
    model_rows = jnp.concatenate([turned(x, 1) for x in server[:3]])

    ids = token_ids[0]
    all_ids = [ids] + [None] * (size - 1)
    for j in range(1, size):
        back = 2 * (-(j // 2) % (size // 2)) + j % 2
        all_ids[back] = lax.ppermute(ids, "fsdp", [(i, peer(i, j, size)) for i in range(size)])
    slabs = gathered(model_rows, size)
    weights = joined(slabs, 3)
    all_ids, _ = lax.optimization_barrier((jnp.concatenate(all_ids), model_rows))
    looked_up = embedding.at[all_ids].get(mode="promise_in_bounds")

    worker_place = place - place % 2 + core
    order = jnp.stack([peer(worker_place, j, size) for j in range(size)])
    wanted = (order[:, None] * width + jnp.arange(width)[None, :]).reshape(-1)
    reorder = (jnp.arange(size * width)[:, None] == wanted[None, :]).astype(jnp.bfloat16)
    late_target, looked_up = lax.optimization_barrier((target[0], looked_up))
    goal = jnp.dot(moved(late_target, 0), reorder, preferred_element_type=jnp.float32)
    goal = lax.optimization_barrier(goal.astype(jnp.bfloat16))
    gain = jnp.dot(
        norm_gain[None], reorder.astype(jnp.float32), precision=lax.Precision.HIGHEST
    )

    x_size = size // 2
    arrived = [None] * x_size
    for dx in near_first(size):
        both = looked_up[2 * dx * tok_rows : 2 * (dx + 1) * tok_rows]
        arrived[-dx % x_size] = moved(both, dx)
    theirs = swapped_cores(jnp.stack([a[tok_rows:] for a in arrived]))
    pieces = [p for dx in range(x_size) for p in (arrived[dx][:tok_rows], theirs[dx])]
    stacked = lax.optimization_barrier(jnp.stack(pieces))
    embedded = jnp.moveaxis(stacked, 0, 1).reshape(tok_rows, size * width)
    widened = embedded.astype(jnp.float32)
    inv_norm = lax.rsqrt(jnp.mean(widened * widened, axis=1, keepdims=True) + norm_eps)
    normed = (widened * inv_norm * gain).astype(jnp.bfloat16)
    residual = widened - goal.astype(jnp.float32)

    control_rows = jnp.concatenate([turned(x, 1) for x in server[3:]])
    client_index = lax.axis_index("clients")
    slots = jnp.arange(local_steps.shape[0])
    step_count = jnp.sum(jnp.where(slots == client_index, local_steps, 0)).astype(jnp.float32)
    own_weight = jnp.sum(jnp.where(slots == client_index, client_weight, 0)).astype(jnp.float32)
    weight_total = jnp.sum(client_weight).astype(jnp.float32)
    second = (step_count > 1.5).astype(jnp.float32)
    own_control = client_control[0].reshape(control_rows.shape)
    correction = control_rows.astype(jnp.float32) - own_control

    grads = summed_terms(local_grads(normed, residual, weights, loss_scale), size)
    current = (
        model_rows.astype(jnp.float32) - learning_rate * (grads + correction)
    ).astype(jnp.bfloat16)
    slabs = gathered(current, size)
    weights = joined(slabs, 3)

    count = local_steps.shape[0] // 2
    for_step = (own_weight * (grads + step_count * correction)).astype(jnp.bfloat16)
    for_control = (own_weight / step_count * grads).astype(jnp.bfloat16)
    for_step, for_control, _ = lax.optimization_barrier((for_step, for_control, slabs[0]))
    early = [
        [cut_for_clients(x, count) for x in jnp.split(part, 3)] for part in (for_step, for_control)
    ]
    normed, early = lax.optimization_barrier((normed, early))
    last = second * summed_terms(local_grads(normed, residual, weights, loss_scale), size)
    late = [cut_for_clients(x, count) for x in jnp.split((own_weight * last).astype(jnp.bfloat16), 3)]
    sums = sum_clients(
        [
            (e.astype(jnp.float32) + share * l.astype(jnp.float32)).astype(jnp.bfloat16)
            for part, share in zip(early, (1.0, 0.5))
            for e, l in zip(part, late)
        ]
    )
    update = ((grads + last) / step_count).reshape(client_control.shape)
    steps_total = jnp.sum(local_steps * client_weight).astype(jnp.float32)
    rounded_away = global_control - global_control.astype(jnp.bfloat16).astype(jnp.float32)
    server_step = (sums[:3] + steps_total * rounded_away) / weight_total
    server_control = sums[3:] / weight_total
    return (server_step, server_control, update)


def solution(mesh):
    placed = (
        P("clients", "fsdp"),
        P("clients", "fsdp", None),
        P(None, "fsdp"),
        P(),
        P(None, "fsdp", "clients"),
        P(None, "fsdp", "clients"),
        P("clients", None, "fsdp", None),
        P(),
        P(),
    )
    return jax.shard_map(
        body,
        mesh=mesh,
        in_specs=placed,
        out_specs=(
            P(None, "fsdp", "clients"),
            P(None, "fsdp", "clients"),
            P("clients", None, "fsdp", None),
        ),
        check_vma=False,
    )
```

```python
import math

import jax
import jax.numpy as jnp
from jax import lax
from jax.sharding import PartitionSpec as P

LOCAL = 2


learning_rate = 0.005
norm_eps = 1e-06


BOTH = ("clients", "fsdp")


def moved(block, dx):
    clients, size = lax.axis_size("clients"), lax.axis_size("fsdp")
    pairs = []
    for client in range(clients):
        for place in range(size):
            x = (place // 2 + dx) % (size // 2)
            z, core = place % 2, client % 2
            target = (client - core + z) * size + 2 * x + core
            pairs.append((client * size + place, target))
    return lax.ppermute(block, BOTH, pairs)


def peer(place, offset, size):
    x_size = size // 2
    return ((place // 2 + offset // 2) % x_size) * 2 + ((place % 2) ^ (offset % 2))


def near_first(size):
    x_size = size // 2
    return sorted(range(x_size), key=lambda dx: min(dx, x_size - dx))


def swapped_cores(x):
    return lax.ppermute(x, "clients", [(i, i ^ 1) for i in range(lax.axis_size("clients"))])


def gathered(block, size):
    x_size = size // 2
    arrived = [None] * size
    for dx in near_first(size):
        back = 2 * (-dx % x_size)
        arrived[back] = moved(block, dx)
    for dx in near_first(size):
        back = 2 * (-dx % x_size)
        arrived[back + 1] = swapped_cores(arrived[back])
    return arrived


def summed(blocks):
    size = len(blocks)
    pairs = [
        (
            blocks[2 * dx].astype(jnp.float32)
            + swapped_cores(blocks[2 * dx + 1]).astype(jnp.float32)
        ).astype(jnp.bfloat16)
        for dx in range(size // 2)
    ]
    arrived = [moved(pairs[dx], dx) for dx in near_first(size)[::-1]]
    return sum(a.astype(jnp.float32) for a in arrived)


def client_place():
    index = lax.axis_index("clients")
    return index // 8, index // 2 % 4


def client_shifted(x, high, y):
    pairs = []
    for i in range(lax.axis_size("clients")):
        pairs.append((i, (i // 8 + high) % 4 * 8 + (i // 2 + y) % 4 * 2 + i % 2))
    return lax.ppermute(x, "clients", pairs)


def collected(block, step, place):
    arrived = [block] + [None] * 3
    for k in range(1, 4):
        arrived[4 - k] = client_shifted(block, k * step[0], k * step[1])
    twice = jnp.stack(arrived + arrived)
    return lax.dynamic_slice_in_dim(twice, (4 - place) % 4, 4)


def reduced(blocks, step, place):
    own = lax.dynamic_index_in_dim(blocks, place, 0, False)
    came = [
        client_shifted(
            lax.dynamic_index_in_dim(blocks, (place + k) % 4, 0, False), k * step[0], k * step[1]
        )
        for k in range(1, 4)
    ]
    return sum(c.astype(jnp.float32) for c in [own] + came)


def turned(x, contract):
    eye = jnp.eye(x.shape[contract], dtype=x.dtype)
    dims = (((1,), (1,)), ((), ())) if contract else (((0,), (0,)), ((), ()))
    both = (eye, x) if contract else (x, eye)
    return lax.dot_general(*both, dims, preferred_element_type=jnp.float32).astype(x.dtype)


def start_gather_clients(x):
    a, rows, cols = x.shape
    return collected(jnp.swapaxes(x, 1, 2).reshape(a * cols, rows), (0, 1), client_place()[1])


def end_gather_clients(mine, a):
    count, wide, rows = mine.shape
    cols = wide // a
    theirs = swapped_cores(mine)
    first = lax.axis_index("clients") % 2 == 0
    both = jnp.stack([jnp.where(first, mine, theirs), jnp.where(first, theirs, mine)], axis=1)
    both = both.reshape(count, 2, a, cols, rows)
    return [both[:, :, k].reshape(count * 2 * cols, rows) for k in range(a)]


def cut_for_clients(array, count):
    rows, cols = array.shape
    return turned(array, 0).reshape(count, 2, cols // (2 * count), rows)


def sum_clients(cuts):
    count, _, part, rows = cuts[0].shape
    a = len(cuts)
    cut = jnp.stack(cuts, axis=2).reshape(count, 2, a * part, rows)
    core = lax.axis_index("clients") % 2
    kept = lax.dynamic_index_in_dim(cut, core, 1, keepdims=False)
    given = lax.dynamic_index_in_dim(cut, 1 - core, 1, keepdims=False)
    came = swapped_cores(given)
    pair = (kept.astype(jnp.float32) + came.astype(jnp.float32)).astype(jnp.bfloat16)
    high, y = client_place()
    pair = jnp.moveaxis(pair.reshape(4, 4, a * part, rows), 1, 0)
    line = reduced(pair, (0, 1), y).astype(jnp.bfloat16)
    total = reduced(line, (1, 0), high)
    return jnp.swapaxes(total.reshape(a, part, rows), 1, 2)


def gelu_pair(pre_act):
    return jax.vjp(lambda inputs: jax.nn.gelu(inputs, approximate=True), pre_act)


def contract_rows(left, right):
    return lax.dot_general(
        left, right, (((0,), (0,)), ((), ())), preferred_element_type=jnp.float32
    )


def local_grads(normed, residual, weights, loss_scale):
    gate_w, up_w, out_w = weights
    gate_pre = jnp.dot(normed, gate_w, preferred_element_type=jnp.float32)
    up_pre = jnp.dot(normed, up_w, preferred_element_type=jnp.float32)
    gate_act, gelu_back = gelu_pair(gate_pre)
    hidden = (gate_act * up_pre).astype(jnp.bfloat16)
    projected = lax.dot_general(
        hidden, out_w, (((1,), (1,)), ((), ())), preferred_element_type=jnp.float32
    )
    out_grad = ((residual + projected) * loss_scale).astype(jnp.bfloat16)
    hidden_grad = jnp.dot(out_grad, out_w, preferred_element_type=jnp.float32)
    gate_grad = gelu_back(hidden_grad * up_pre)[0].astype(jnp.bfloat16)
    up_grad = (hidden_grad * gate_act).astype(jnp.bfloat16)
    return [
        contract_rows(normed, gate_grad).astype(jnp.bfloat16),
        contract_rows(normed, up_grad).astype(jnp.bfloat16),
        contract_rows(out_grad, hidden).astype(jnp.bfloat16),
    ]


def summed_terms(terms, size):
    rows = terms[0].shape[0] // size
    return summed(
        [jnp.concatenate([t[j * rows : (j + 1) * rows] for t in terms]) for j in range(size)]
    )


def joined(pieces, count):
    rows = pieces[0].shape[0] // count
    return [
        jnp.concatenate([p[k * rows : (k + 1) * rows] for p in pieces]) for k in range(count)
    ]


def body(
    token_ids,
    target,
    embedding,
    norm_gain,
    global_model,
    global_control,
    client_control,
    local_steps,
    client_weight,
):
    size = lax.axis_size("fsdp")
    place = lax.axis_index("fsdp")
    core = lax.axis_index("clients") % 2
    width = embedding.shape[1]
    tok_rows = target.shape[1]
    loss_scale = 1.0 / math.sqrt(tok_rows * size)

    line = start_gather_clients(
        jnp.concatenate([global_model, global_control]).astype(jnp.bfloat16)
    )

    all_ids = lax.all_to_all(
        jnp.broadcast_to(token_ids, (size, tok_rows)), "fsdp", 0, 0, tiled=True
    )
    all_ids, line = lax.optimization_barrier((all_ids, line))
    looked_up = embedding.at[all_ids.reshape(-1)].get(mode="promise_in_bounds")
    plane = collected(line, (1, 0), client_place()[0])
    looked_up, plane = lax.optimization_barrier((looked_up, plane))
    server = end_gather_clients(plane.reshape(-1, *plane.shape[2:]), 6)
    model_rows = jnp.concatenate([turned(x, 1) for x in server[:3]])
    weights = joined(gathered(model_rows, size), 3)

    worker_place = place - place % 2 + core
    order = jnp.stack([peer(worker_place, j, size) for j in range(size)])
    wanted = (order[:, None] * width + jnp.arange(width)[None, :]).reshape(-1)
    reorder = (jnp.arange(size * width)[:, None] == wanted[None, :]).astype(jnp.bfloat16)
    late_target, looked_up = lax.optimization_barrier((target[0], looked_up))
    goal = jnp.dot(moved(late_target, 0), reorder, preferred_element_type=jnp.float32)
    goal = lax.optimization_barrier(goal.astype(jnp.bfloat16))
    gain = jnp.dot(
        norm_gain[None], reorder.astype(jnp.float32), precision=lax.Precision.HIGHEST
    )

    x_size = size // 2
    x = place // 2
    arrived = [None] * x_size
    for dx in near_first(size):
        both = lax.dynamic_slice_in_dim(
            looked_up, (x + dx) % x_size * 2 * tok_rows, 2 * tok_rows
        )
        arrived[-dx % x_size] = moved(both, dx)
    arrived, model_rows = lax.optimization_barrier((arrived, model_rows))
    arrived = jnp.stack(arrived).reshape(x_size, 2, tok_rows, width)
    ours = lax.dynamic_index_in_dim(arrived, core, 1, False)
    theirs = swapped_cores(lax.dynamic_index_in_dim(arrived, 1 - core, 1, False))
    pieces = [p for dx in range(x_size) for p in (ours[dx], theirs[dx])]
    stacked = lax.optimization_barrier(jnp.stack(pieces))
    embedded = jnp.moveaxis(stacked, 0, 1).reshape(tok_rows, size * width)
    widened = embedded.astype(jnp.float32)
    inv_norm = lax.rsqrt(jnp.mean(widened * widened, axis=1, keepdims=True) + norm_eps)
    normed = (widened * inv_norm * gain).astype(jnp.bfloat16)
    residual = widened - goal.astype(jnp.float32)

    control_rows = jnp.concatenate([turned(x, 1) for x in server[3:]])
    client_index = lax.axis_index("clients")
    slots = jnp.arange(local_steps.shape[0])
    step_count = jnp.sum(jnp.where(slots == client_index, local_steps, 0)).astype(jnp.float32)
    own_weight = jnp.sum(jnp.where(slots == client_index, client_weight, 0)).astype(jnp.float32)
    weight_total = jnp.sum(client_weight).astype(jnp.float32)
    second = (step_count > 1.5).astype(jnp.float32)
    own_control = client_control[0].reshape(control_rows.shape)
    correction = control_rows.astype(jnp.float32) - own_control

    grads = summed_terms(local_grads(normed, residual, weights, loss_scale), size)
    current = (
        model_rows.astype(jnp.float32) - learning_rate * (grads + correction)
    ).astype(jnp.bfloat16)
    slabs = gathered(current, size)
    weights = joined(slabs, 3)

    count = local_steps.shape[0] // 2
    for_step = (own_weight * (grads + step_count * correction)).astype(jnp.bfloat16)
    for_control = (own_weight / step_count * grads).astype(jnp.bfloat16)
    for_step, for_control, _ = lax.optimization_barrier((for_step, for_control, slabs[0]))
    early = [
        [cut_for_clients(x, count) for x in jnp.split(part, 3)] for part in (for_step, for_control)
    ]
    normed, early = lax.optimization_barrier((normed, early))
    last = second * summed_terms(local_grads(normed, residual, weights, loss_scale), size)
    late = [cut_for_clients(x, count) for x in jnp.split((own_weight * last).astype(jnp.bfloat16), 3)]
    sums = sum_clients(
        [
            (e.astype(jnp.float32) + share * l.astype(jnp.float32)).astype(jnp.bfloat16)
            for part, share in zip(early, (1.0, 0.5))
            for e, l in zip(part, late)
        ]
    )
    update = ((grads + last) / step_count).reshape(client_control.shape)
    steps_total = jnp.sum(local_steps * client_weight).astype(jnp.float32)
    rounded_away = global_control - global_control.astype(jnp.bfloat16).astype(jnp.float32)
    server_step = (sums[:3] + steps_total * rounded_away) / weight_total
    server_control = sums[3:] / weight_total
    return (server_step, server_control, update)


def solution(mesh):
    placed = (
        P("clients", "fsdp"),
        P("clients", "fsdp", None),
        P(None, "fsdp"),
        P(),
        P(None, "fsdp", "clients"),
        P(None, "fsdp", "clients"),
        P("clients", None, "fsdp", None),
        P(),
        P(),
    )
    return jax.shard_map(
        body,
        mesh=mesh,
        in_specs=placed,
        out_specs=(
            P(None, "fsdp", "clients"),
            P(None, "fsdp", "clients"),
            P("clients", None, "fsdp", None),
        ),
        check_vma=False,
    )
```

```python
import math

import jax
import jax.numpy as jnp
from jax import lax
from jax.experimental import pallas as pl
from jax.experimental.pallas import tpu as pltpu
from jax.sharding import PartitionSpec as P

LOCAL = 2


learning_rate = 0.005
norm_eps = 1e-06


BOTH = ("clients", "fsdp")


def moved(block, dx):
    clients, size = lax.axis_size("clients"), lax.axis_size("fsdp")
    pairs = []
    for client in range(clients):
        for place in range(size):
            x = (place // 2 + dx) % (size // 2)
            z, core = place % 2, client % 2
            target = (client - core + z) * size + 2 * x + core
            pairs.append((client * size + place, target))
    return lax.ppermute(block, BOTH, pairs)


def peer(place, offset, size):
    x_size = size // 2
    return ((place // 2 + offset // 2) % x_size) * 2 + ((place % 2) ^ (offset % 2))


def near_first(size):
    x_size = size // 2
    return sorted(range(x_size), key=lambda dx: min(dx, x_size - dx))


def swapped_cores(x):
    return lax.ppermute(x, "clients", [(i, i ^ 1) for i in range(lax.axis_size("clients"))])


def gathered(block, size):
    x_size = size // 2
    arrived = [None] * size
    for dx in near_first(size):
        back = 2 * (-dx % x_size)
        arrived[back] = moved(block, dx)
    for dx in near_first(size):
        back = 2 * (-dx % x_size)
        arrived[back + 1] = swapped_cores(arrived[back])
    return arrived


def summed(blocks):
    size = len(blocks)
    pairs = [
        (
            blocks[2 * dx].astype(jnp.float32)
            + swapped_cores(blocks[2 * dx + 1]).astype(jnp.float32)
        ).astype(jnp.bfloat16)
        for dx in range(size // 2)
    ]
    arrived = [moved(pairs[dx], dx) for dx in near_first(size)[::-1]]
    return sum(a.astype(jnp.float32) for a in arrived)


def client_place():
    index = lax.axis_index("clients")
    return index // 8, index // 2 % 4


def client_shifted(x, high, y):
    pairs = []
    for i in range(lax.axis_size("clients")):
        pairs.append((i, (i // 8 + high) % 4 * 8 + (i // 2 + y) % 4 * 2 + i % 2))
    return lax.ppermute(x, "clients", pairs)


def collected(block, step, place):
    arrived = [block] + [None] * 3
    for k in range(1, 4):
        arrived[4 - k] = client_shifted(block, k * step[0], k * step[1])
    twice = jnp.stack(arrived + arrived)
    return lax.dynamic_slice_in_dim(twice, (4 - place) % 4, 4)


def reduced(blocks, step, place):
    own = lax.dynamic_index_in_dim(blocks, place, 0, False)
    came = [
        client_shifted(
            lax.dynamic_index_in_dim(blocks, (place + k) % 4, 0, False), k * step[0], k * step[1]
        )
        for k in range(1, 4)
    ]
    return sum(c.astype(jnp.float32) for c in [own] + came)


def turned(x, contract):
    eye = jnp.eye(x.shape[contract], dtype=x.dtype)
    dims = (((1,), (1,)), ((), ())) if contract else (((0,), (0,)), ((), ()))
    both = (eye, x) if contract else (x, eye)
    return lax.dot_general(*both, dims, preferred_element_type=jnp.float32).astype(x.dtype)


def start_gather_clients(x):
    a, rows, cols = x.shape
    return collected(jnp.swapaxes(x, 1, 2).reshape(a * cols, rows), (0, 1), client_place()[1])


def end_gather_clients(mine, a):
    count, wide, rows = mine.shape
    cols = wide // a
    theirs = swapped_cores(mine)
    first = lax.axis_index("clients") % 2 == 0
    both = jnp.stack([jnp.where(first, mine, theirs), jnp.where(first, theirs, mine)], axis=1)
    both = both.reshape(count, 2, a, cols, rows)
    return [both[:, :, k].reshape(count * 2 * cols, rows) for k in range(a)]


def cut_for_clients(array, count):
    rows, cols = array.shape
    return turned(array, 0).reshape(count, 2, cols // (2 * count), rows)


def sum_clients(cuts):
    count, _, part, rows = cuts[0].shape
    a = len(cuts)
    cut = jnp.stack(cuts, axis=2).reshape(count, 2, a * part, rows)
    core = lax.axis_index("clients") % 2
    kept = lax.dynamic_index_in_dim(cut, core, 1, keepdims=False)
    given = lax.dynamic_index_in_dim(cut, 1 - core, 1, keepdims=False)
    came = swapped_cores(given)
    pair = (kept.astype(jnp.float32) + came.astype(jnp.float32)).astype(jnp.bfloat16)
    high, y = client_place()
    pair = jnp.moveaxis(pair.reshape(4, 4, a * part, rows), 1, 0)
    line = reduced(pair, (0, 1), y).astype(jnp.bfloat16)
    total = reduced(line, (1, 0), high)
    return jnp.swapaxes(total.reshape(a, part, rows), 1, 2)


GELU_SCALE = math.sqrt(2.0 / math.pi)
GELU_CUBE = 0.044715
TILES = 2


def dot(left, right, left_dim, right_dim):
    dims = (((left_dim,), (right_dim,)), ((), ()))
    return lax.dot_general(left, right, dims, preferred_element_type=jnp.float32)


def step_kernel(size, loss_scale, *refs):
    slabs, (normed, residual), blocks = refs[:size], refs[size : size + 2], refs[size + 2 : -6]
    gate_w, up_w, out_w, hidden, gate_grad, up_grad = refs[-6:]
    rows = slabs[0].shape[0] // 3
    width = rows * size
    for j, slab in enumerate(slabs):
        for k, weights in enumerate((gate_w, up_w, out_w)):
            weights[j * rows : (j + 1) * rows, :] = slab[k * rows : (k + 1) * rows, :]
    tile = normed.shape[0] // TILES
    for t in range(TILES):
        part = pl.ds(t * tile, tile)
        inputs = normed[part, :]
        gate_pre = dot(inputs, gate_w[...], 1, 0)
        up_pre = dot(inputs, up_w[...], 1, 0)
        square = gate_pre * gate_pre
        tanh = jnp.tanh(GELU_SCALE * gate_pre * (1.0 + GELU_CUBE * square))
        half = 0.5 + 0.5 * tanh
        slope = half + gate_pre * (0.5 - 0.5 * tanh * tanh) * (
            GELU_SCALE + (3.0 * GELU_CUBE * GELU_SCALE) * square
        )
        gate_act = gate_pre * half
        hidden_part = (gate_act * up_pre).astype(jnp.bfloat16)
        hidden[part, :] = hidden_part
        projected = dot(hidden_part, out_w[...], 1, 1)
        out_part = ((residual[part, :] + projected) * loss_scale).astype(jnp.bfloat16)
        residual[part, :] = out_part.astype(jnp.float32)
        hidden_grad = dot(out_part, out_w[...], 1, 0)
        gate_grad[part, :] = (hidden_grad * up_pre * slope).astype(jnp.bfloat16)
        up_grad[part, :] = (hidden_grad * gate_act).astype(jnp.bfloat16)
    each = width // 2
    for k, (left, right) in enumerate(((residual, hidden), (normed, gate_grad), (normed, up_grad))):
        k = (k + 2) % 3
        for h in range(2):
            columns = left[:, h * each : (h + 1) * each].astype(jnp.bfloat16)
            term = dot(columns, right[...], 0, 0).astype(jnp.bfloat16)
            for j in range(size // 2):
                blocks[h * (size // 2) + j][k * rows : (k + 1) * rows, :] = term[
                    j * rows : (j + 1) * rows
                ]


def local_terms(normed, residual, slabs, loss_scale):
    size = len(slabs)
    tokens, width = normed.shape
    hidden_size = slabs[0].shape[1]
    vmem = pl.BlockSpec(memory_space=pltpu.VMEM)

    def kernel(*refs):
        ins, outs, (copied, *scratch) = refs[: size + 2], refs[size + 2 : 2 * size + 2], refs[2 * size + 2 :]
        copied[...] = ins[size + 1][...]
        step_kernel(size, loss_scale, *ins[: size + 1], copied, *outs, *scratch)

    return list(
        pl.pallas_call(
            kernel,
            out_shape=[jax.ShapeDtypeStruct(slabs[0].shape, jnp.bfloat16)] * size,
            in_specs=[vmem] * (size + 2),
            out_specs=[vmem] * size,
            scratch_shapes=[pltpu.VMEM((tokens, width), jnp.float32)]
            + [pltpu.VMEM((width, hidden_size), jnp.bfloat16)] * 3
            + [pltpu.VMEM((tokens, hidden_size), jnp.bfloat16)] * 3,
            compiler_params=pltpu.CompilerParams(vmem_limit_bytes=52 * 2**20),
            cost_estimate=pl.CostEstimate(
                flops=12 * tokens * width * hidden_size,
                transcendentals=tokens * hidden_size,
                bytes_accessed=12 * width * hidden_size,
            ),
        )(*slabs, normed, residual)
    )


def body(
    token_ids,
    target,
    embedding,
    norm_gain,
    global_model,
    global_control,
    client_control,
    local_steps,
    client_weight,
):
    size = lax.axis_size("fsdp")
    place = lax.axis_index("fsdp")
    core = lax.axis_index("clients") % 2
    width = embedding.shape[1]
    tok_rows = target.shape[1]
    loss_scale = 1.0 / math.sqrt(tok_rows * size)

    line = start_gather_clients(
        jnp.concatenate([global_model, global_control]).astype(jnp.bfloat16)
    )

    all_ids = lax.all_to_all(
        jnp.broadcast_to(token_ids, (size, tok_rows)), "fsdp", 0, 0, tiled=True
    )
    all_ids, line = lax.optimization_barrier((all_ids, line))
    looked_up = embedding.at[all_ids.reshape(-1)].get(mode="promise_in_bounds")
    plane = collected(line, (1, 0), client_place()[0])
    looked_up, plane = lax.optimization_barrier((looked_up, plane))
    server = end_gather_clients(plane.reshape(-1, *plane.shape[2:]), 6)
    model_rows = jnp.concatenate([turned(x, 1) for x in server[:3]])
    slabs = gathered(model_rows, size)

    worker_place = place - place % 2 + core
    order = jnp.stack([peer(worker_place, j, size) for j in range(size)])
    wanted = (order[:, None] * width + jnp.arange(width)[None, :]).reshape(-1)
    reorder = (jnp.arange(size * width)[:, None] == wanted[None, :]).astype(jnp.bfloat16)
    late_target, looked_up = lax.optimization_barrier((target[0], looked_up))
    goal = jnp.dot(moved(late_target, 0), reorder, preferred_element_type=jnp.float32)
    goal = lax.optimization_barrier(goal.astype(jnp.bfloat16))
    gain = jnp.dot(
        norm_gain[None], reorder.astype(jnp.float32), precision=lax.Precision.HIGHEST
    )

    x_size = size // 2
    x = place // 2
    arrived = [None] * x_size
    for dx in near_first(size):
        both = lax.dynamic_slice_in_dim(
            looked_up, (x + dx) % x_size * 2 * tok_rows, 2 * tok_rows
        )
        arrived[-dx % x_size] = moved(both, dx)
    arrived, model_rows = lax.optimization_barrier((arrived, model_rows))
    arrived = jnp.stack(arrived).reshape(x_size, 2, tok_rows, width)
    ours = lax.dynamic_index_in_dim(arrived, core, 1, False)
    theirs = swapped_cores(lax.dynamic_index_in_dim(arrived, 1 - core, 1, False))
    pieces = [p for dx in range(x_size) for p in (ours[dx], theirs[dx])]
    stacked = lax.optimization_barrier(jnp.stack(pieces))
    embedded = jnp.moveaxis(stacked, 0, 1).reshape(tok_rows, size * width)
    widened = embedded.astype(jnp.float32)
    inv_norm = lax.rsqrt(jnp.mean(widened * widened, axis=1, keepdims=True) + norm_eps)
    normed = (widened * inv_norm * gain).astype(jnp.bfloat16)
    residual = widened - goal.astype(jnp.float32)

    control_rows = jnp.concatenate([turned(x, 1) for x in server[3:]])
    client_index = lax.axis_index("clients")
    slots = jnp.arange(local_steps.shape[0])
    step_count = jnp.sum(jnp.where(slots == client_index, local_steps, 0)).astype(jnp.float32)
    own_weight = jnp.sum(jnp.where(slots == client_index, client_weight, 0)).astype(jnp.float32)
    weight_total = jnp.sum(client_weight).astype(jnp.float32)
    second = (step_count > 1.5).astype(jnp.float32)
    own_control = client_control[0].reshape(control_rows.shape)
    correction = control_rows.astype(jnp.float32) - own_control

    grads = summed(local_terms(normed, residual, slabs, loss_scale))
    current = (
        model_rows.astype(jnp.float32) - learning_rate * (grads + correction)
    ).astype(jnp.bfloat16)
    slabs = gathered(current, size)

    count = local_steps.shape[0] // 2
    for_step = (own_weight * (grads + step_count * correction)).astype(jnp.bfloat16)
    for_control = (own_weight / step_count * grads).astype(jnp.bfloat16)
    for_step, for_control, _ = lax.optimization_barrier((for_step, for_control, slabs[0]))
    early = [
        [cut_for_clients(x, count) for x in jnp.split(part, 3)] for part in (for_step, for_control)
    ]
    normed, early = lax.optimization_barrier((normed, early))
    last = second * summed(local_terms(normed, residual, slabs, loss_scale))
    late = [cut_for_clients(x, count) for x in jnp.split((own_weight * last).astype(jnp.bfloat16), 3)]
    sums = sum_clients(
        [
            (e.astype(jnp.float32) + share * l.astype(jnp.float32)).astype(jnp.bfloat16)
            for part, share in zip(early, (1.0, 0.5))
            for e, l in zip(part, late)
        ]
    )
    update = ((grads + last) / step_count).reshape(client_control.shape)
    steps_total = jnp.sum(local_steps * client_weight).astype(jnp.float32)
    rounded_away = global_control - global_control.astype(jnp.bfloat16).astype(jnp.float32)
    server_step = (sums[:3] + steps_total * rounded_away) / weight_total
    server_control = sums[3:] / weight_total
    return (server_step, server_control, update)


def solution(mesh):
    placed = (
        P("clients", "fsdp"),
        P("clients", "fsdp", None),
        P(None, "fsdp"),
        P(),
        P(None, "fsdp", "clients"),
        P(None, "fsdp", "clients"),
        P("clients", None, "fsdp", None),
        P(),
        P(),
    )
    return jax.shard_map(
        body,
        mesh=mesh,
        in_specs=placed,
        out_specs=(
            P(None, "fsdp", "clients"),
            P(None, "fsdp", "clients"),
            P("clients", None, "fsdp", None),
        ),
        check_vma=False,
    )
```

```python
import math

import jax
import jax.numpy as jnp
from jax import lax
from jax.experimental import pallas as pl
from jax.experimental.pallas import tpu as pltpu
from jax.sharding import PartitionSpec as P

LOCAL = 2


learning_rate = 0.005
norm_eps = 1e-06


BOTH = ("clients", "fsdp")


def moved(block, dx):
    clients, size = lax.axis_size("clients"), lax.axis_size("fsdp")
    pairs = []
    for client in range(clients):
        for place in range(size):
            x = (place // 2 + dx) % (size // 2)
            z, core = place % 2, client % 2
            target = (client - core + z) * size + 2 * x + core
            pairs.append((client * size + place, target))
    return lax.ppermute(block, BOTH, pairs)


def peer(place, offset, size):
    x_size = size // 2
    return ((place // 2 + offset // 2) % x_size) * 2 + ((place % 2) ^ (offset % 2))


def near_first(size):
    x_size = size // 2
    return sorted(range(x_size), key=lambda dx: min(dx, x_size - dx))


def swapped_cores(x):
    return lax.ppermute(x, "clients", [(i, i ^ 1) for i in range(lax.axis_size("clients"))])


def gathered(block, size):
    x_size = size // 2
    arrived = [None] * size
    for dx in near_first(size):
        back = 2 * (-dx % x_size)
        arrived[back] = moved(block, dx)
    for dx in near_first(size):
        back = 2 * (-dx % x_size)
        arrived[back + 1] = swapped_cores(arrived[back])
    return arrived


def summed(blocks):
    size = len(blocks)
    pairs = [
        (
            blocks[2 * dx].astype(jnp.float32)
            + swapped_cores(blocks[2 * dx + 1]).astype(jnp.float32)
        ).astype(jnp.bfloat16)
        for dx in range(size // 2)
    ]
    arrived = [moved(pairs[dx], dx) for dx in near_first(size)[::-1]]
    return sum(a.astype(jnp.float32) for a in arrived)


def client_place():
    index = lax.axis_index("clients")
    return index // 8, index // 2 % 4


def client_shifted(x, high, y):
    pairs = []
    for i in range(lax.axis_size("clients")):
        pairs.append((i, (i // 8 + high) % 4 * 8 + (i // 2 + y) % 4 * 2 + i % 2))
    return lax.ppermute(x, "clients", pairs)


def collected(block, step, place):
    arrived = [block] + [None] * 3
    for k in range(1, 4):
        arrived[4 - k] = client_shifted(block, k * step[0], k * step[1])
    twice = jnp.stack(arrived + arrived)
    return lax.dynamic_slice_in_dim(twice, (4 - place) % 4, 4)


def reduced(blocks, step, place):
    own = lax.dynamic_index_in_dim(blocks, place, 0, False)
    came = [
        client_shifted(
            lax.dynamic_index_in_dim(blocks, (place + k) % 4, 0, False), k * step[0], k * step[1]
        )
        for k in range(1, 4)
    ]
    return sum(c.astype(jnp.float32) for c in [own] + came)


def turned(x, contract):
    eye = jnp.eye(x.shape[contract], dtype=x.dtype)
    dims = (((1,), (1,)), ((), ())) if contract else (((0,), (0,)), ((), ()))
    both = (eye, x) if contract else (x, eye)
    return lax.dot_general(*both, dims, preferred_element_type=jnp.float32).astype(x.dtype)


def start_gather_clients(x):
    a, rows, cols = x.shape
    return collected(jnp.swapaxes(x, 1, 2).reshape(a * cols, rows), (0, 1), client_place()[1])


def end_gather_clients(mine, a):
    count, wide, rows = mine.shape
    cols = wide // a
    theirs = swapped_cores(mine)
    first = lax.axis_index("clients") % 2 == 0
    both = jnp.stack([jnp.where(first, mine, theirs), jnp.where(first, theirs, mine)], axis=1)
    both = both.reshape(count, 2, a, cols, rows)
    return [both[:, :, k].reshape(count * 2 * cols, rows) for k in range(a)]


def cut_for_clients(array, count):
    rows, cols = array.shape
    return turned(array, 0).reshape(count, 2, cols // (2 * count), rows)


def paired(cuts):
    count, _, part, rows = cuts[0].shape
    cut = jnp.stack(cuts, axis=2).reshape(count, 2, len(cuts) * part, rows)
    core = lax.axis_index("clients") % 2
    kept = lax.dynamic_index_in_dim(cut, core, 1, keepdims=False)
    given = lax.dynamic_index_in_dim(cut, 1 - core, 1, keepdims=False)
    came = swapped_cores(given)
    pair = (kept.astype(jnp.float32) + came.astype(jnp.float32)).astype(jnp.bfloat16)
    return jnp.moveaxis(pair.reshape(4, 4, len(cuts) * part, rows), 1, 0)


GELU_SCALE = math.sqrt(2.0 / math.pi)
GELU_CUBE = 0.044715
TILES = 2


def dot(left, right, left_dim, right_dim):
    dims = (((left_dim,), (right_dim,)), ((), ()))
    return lax.dot_general(left, right, dims, preferred_element_type=jnp.float32)


def step_kernel(size, loss_scale, *refs):
    slabs, (normed, residual), blocks = refs[:size], refs[size : size + 2], refs[size + 2 : -6]
    gate_w, up_w, out_w, hidden, gate_grad, up_grad = refs[-6:]
    rows = slabs[0].shape[0] // 3
    width = rows * size
    for j, slab in enumerate(slabs):
        for k, weights in enumerate((gate_w, up_w, out_w)):
            weights[j * rows : (j + 1) * rows, :] = slab[k * rows : (k + 1) * rows, :]
    tile = normed.shape[0] // TILES
    for t in range(TILES):
        part = pl.ds(t * tile, tile)
        inputs = normed[part, :]
        gate_pre = dot(inputs, gate_w[...], 1, 0)
        up_pre = dot(inputs, up_w[...], 1, 0)
        square = gate_pre * gate_pre
        tanh = jnp.tanh(GELU_SCALE * gate_pre * (1.0 + GELU_CUBE * square))
        half = 0.5 + 0.5 * tanh
        slope = half + gate_pre * (0.5 - 0.5 * tanh * tanh) * (
            GELU_SCALE + (3.0 * GELU_CUBE * GELU_SCALE) * square
        )
        gate_act = gate_pre * half
        hidden_part = (gate_act * up_pre).astype(jnp.bfloat16)
        hidden[part, :] = hidden_part
        projected = dot(hidden_part, out_w[...], 1, 1)
        out_part = ((residual[part, :] + projected) * loss_scale).astype(jnp.bfloat16)
        residual[part, :] = out_part.astype(jnp.float32)
        hidden_grad = dot(out_part, out_w[...], 1, 0)
        gate_grad[part, :] = (hidden_grad * up_pre * slope).astype(jnp.bfloat16)
        up_grad[part, :] = (hidden_grad * gate_act).astype(jnp.bfloat16)
    each = width // 2
    for k, (left, right) in enumerate(((residual, hidden), (normed, gate_grad), (normed, up_grad))):
        k = (k + 2) % 3
        for h in range(2):
            columns = left[:, h * each : (h + 1) * each].astype(jnp.bfloat16)
            term = dot(columns, right[...], 0, 0).astype(jnp.bfloat16)
            for j in range(size // 2):
                blocks[h * (size // 2) + j][k * rows : (k + 1) * rows, :] = term[
                    j * rows : (j + 1) * rows
                ]


def local_terms(normed, residual, slabs, loss_scale):
    size = len(slabs)
    tokens, width = normed.shape
    hidden_size = slabs[0].shape[1]
    vmem = pl.BlockSpec(memory_space=pltpu.VMEM)

    def kernel(*refs):
        ins, outs, (copied, *scratch) = refs[: size + 2], refs[size + 2 : 2 * size + 2], refs[2 * size + 2 :]
        copied[...] = ins[size + 1][...]
        step_kernel(size, loss_scale, *ins[: size + 1], copied, *outs, *scratch)

    return list(
        pl.pallas_call(
            kernel,
            out_shape=[jax.ShapeDtypeStruct(slabs[0].shape, jnp.bfloat16)] * size,
            in_specs=[vmem] * (size + 2),
            out_specs=[vmem] * size,
            scratch_shapes=[pltpu.VMEM((tokens, width), jnp.float32)]
            + [pltpu.VMEM((width, hidden_size), jnp.bfloat16)] * 3
            + [pltpu.VMEM((tokens, hidden_size), jnp.bfloat16)] * 3,
            compiler_params=pltpu.CompilerParams(vmem_limit_bytes=52 * 2**20),
            cost_estimate=pl.CostEstimate(
                flops=12 * tokens * width * hidden_size,
                transcendentals=tokens * hidden_size,
                bytes_accessed=12 * width * hidden_size,
            ),
        )(*slabs, normed, residual)
    )


def body(
    token_ids,
    target,
    embedding,
    norm_gain,
    global_model,
    global_control,
    client_control,
    local_steps,
    client_weight,
):
    size = lax.axis_size("fsdp")
    place = lax.axis_index("fsdp")
    core = lax.axis_index("clients") % 2
    width = embedding.shape[1]
    tok_rows = target.shape[1]
    loss_scale = 1.0 / math.sqrt(tok_rows * size)

    line = start_gather_clients(
        jnp.concatenate([global_model, global_control]).astype(jnp.bfloat16)
    )

    all_ids = lax.all_to_all(
        jnp.broadcast_to(token_ids, (size, tok_rows)), "fsdp", 0, 0, tiled=True
    )
    all_ids, line = lax.optimization_barrier((all_ids, line))
    looked_up = embedding.at[all_ids.reshape(-1)].get(mode="promise_in_bounds")
    plane = collected(line, (1, 0), client_place()[0])
    looked_up, plane = lax.optimization_barrier((looked_up, plane))
    server = end_gather_clients(plane.reshape(-1, *plane.shape[2:]), 6)
    model_rows = jnp.concatenate([turned(x, 1) for x in server[:3]])
    slabs = gathered(model_rows, size)

    worker_place = place - place % 2 + core
    order = jnp.stack([peer(worker_place, j, size) for j in range(size)])
    wanted = (order[:, None] * width + jnp.arange(width)[None, :]).reshape(-1)
    reorder = (jnp.arange(size * width)[:, None] == wanted[None, :]).astype(jnp.bfloat16)
    late_target, slabs[0] = lax.optimization_barrier((target[0], slabs[0]))
    goal = jnp.dot(moved(late_target, 0), reorder, preferred_element_type=jnp.float32)
    goal = lax.optimization_barrier(goal.astype(jnp.bfloat16))
    gain = jnp.dot(
        norm_gain[None], reorder.astype(jnp.float32), precision=lax.Precision.HIGHEST
    )

    x_size = size // 2
    x = place // 2
    arrived = [None] * x_size
    for dx in near_first(size):
        both = lax.dynamic_slice_in_dim(
            looked_up, (x + dx) % x_size * 2 * tok_rows, 2 * tok_rows
        )
        arrived[-dx % x_size] = moved(both, dx)
    arrived, model_rows = lax.optimization_barrier((arrived, model_rows))
    arrived = jnp.stack(arrived).reshape(x_size, 2, tok_rows, width)
    ours = lax.dynamic_index_in_dim(arrived, core, 1, False)
    theirs = swapped_cores(lax.dynamic_index_in_dim(arrived, 1 - core, 1, False))
    pieces = [p for dx in range(x_size) for p in (ours[dx], theirs[dx])]
    stacked = lax.optimization_barrier(jnp.stack(pieces))
    embedded = jnp.moveaxis(stacked, 0, 1).reshape(tok_rows, size * width)
    widened = embedded.astype(jnp.float32)
    inv_norm = lax.rsqrt(jnp.mean(widened * widened, axis=1, keepdims=True) + norm_eps)
    normed = (widened * inv_norm * gain).astype(jnp.bfloat16)
    residual = widened - goal.astype(jnp.float32)

    control_rows = jnp.concatenate([turned(x, 1) for x in server[3:]])
    client_index = lax.axis_index("clients")
    slots = jnp.arange(local_steps.shape[0])
    step_count = jnp.sum(jnp.where(slots == client_index, local_steps, 0)).astype(jnp.float32)
    own_weight = jnp.sum(jnp.where(slots == client_index, client_weight, 0)).astype(jnp.float32)
    weight_total = jnp.sum(client_weight).astype(jnp.float32)
    second = (step_count > 1.5).astype(jnp.float32)
    own_control = client_control[0].reshape(control_rows.shape)
    correction = control_rows.astype(jnp.float32) - own_control

    grads = summed(local_terms(normed, residual, slabs, loss_scale))
    current = (
        model_rows.astype(jnp.float32) - learning_rate * (grads + correction)
    ).astype(jnp.bfloat16)
    slabs = gathered(current, size)

    count = local_steps.shape[0] // 2
    for_step = (own_weight * (grads + step_count * correction)).astype(jnp.bfloat16)
    for_control = (own_weight / step_count * grads).astype(jnp.bfloat16)
    for_step, for_control, _ = lax.optimization_barrier((for_step, for_control, slabs[0]))
    early = [
        [cut_for_clients(x, count) for x in jnp.split(part, 3)] for part in (for_step, for_control)
    ]
    early = paired([cut for part in early for cut in part])
    normed, early = lax.optimization_barrier((normed, early))
    blocks = local_terms(normed, residual, slabs, loss_scale)
    high, y = client_place()
    early = reduced(early, (0, 1), y)
    blocks, early = lax.optimization_barrier((blocks, early))
    last = second * summed(blocks)
    late = [cut_for_clients(x, count) for x in jnp.split((own_weight * last).astype(jnp.bfloat16), 3)]
    late = reduced(paired(late), (0, 1), y)
    line = (early + jnp.concatenate([late, 0.5 * late], axis=1)).astype(jnp.bfloat16)
    sums = reduced(line, (1, 0), high).reshape(6, -1, line.shape[2])
    sums = jnp.swapaxes(sums, 1, 2)
    update = ((grads + last) / step_count).reshape(client_control.shape)
    steps_total = jnp.sum(local_steps * client_weight).astype(jnp.float32)
    rounded_away = global_control - global_control.astype(jnp.bfloat16).astype(jnp.float32)
    server_step = (sums[:3] + steps_total * rounded_away) / weight_total
    server_control = sums[3:] / weight_total
    return (server_step, server_control, update)


def solution(mesh):
    placed = (
        P("clients", "fsdp"),
        P("clients", "fsdp", None),
        P(None, "fsdp"),
        P(),
        P(None, "fsdp", "clients"),
        P(None, "fsdp", "clients"),
        P("clients", None, "fsdp", None),
        P(),
        P(),
    )
    return jax.shard_map(
        body,
        mesh=mesh,
        in_specs=placed,
        out_specs=(
            P(None, "fsdp", "clients"),
            P(None, "fsdp", "clients"),
            P("clients", None, "fsdp", None),
        ),
        check_vma=False,
    )
```

```python
import math

import jax
import jax.numpy as jnp
from jax import lax
from jax.experimental import pallas as pl
from jax.experimental.pallas import tpu as pltpu
from jax.sharding import PartitionSpec as P

LOCAL = 2


learning_rate = 0.005
norm_eps = 1e-06


BOTH = ("clients", "fsdp")


def moved(block, dx):
    clients, size = lax.axis_size("clients"), lax.axis_size("fsdp")
    pairs = []
    for client in range(clients):
        for place in range(size):
            x = (place // 2 + dx) % (size // 2)
            z, core = place % 2, client % 2
            target = (client - core + z) * size + 2 * x + core
            pairs.append((client * size + place, target))
    return lax.ppermute(block, BOTH, pairs)


def peer(place, offset, size):
    x_size = size // 2
    return ((place // 2 + offset // 2) % x_size) * 2 + ((place % 2) ^ (offset % 2))


def near_first(size):
    x_size = size // 2
    return sorted(range(x_size), key=lambda dx: min(dx, x_size - dx))


def swapped_cores(x):
    return lax.ppermute(x, "clients", [(i, i ^ 1) for i in range(lax.axis_size("clients"))])


def along_x(block, size):
    x_size = size // 2
    arrived = [None] * x_size
    for dx in near_first(size):
        arrived[-dx % x_size] = moved(block, dx)
    return arrived


def with_other_core(arrived):
    slabs = [None] * (2 * len(arrived))
    for dx in near_first(len(slabs)):
        slabs[2 * dx : 2 * dx + 2] = arrived[dx], swapped_cores(arrived[dx])
    return slabs


def summed(blocks):
    size = len(blocks)
    pairs = [
        (
            blocks[2 * dx].astype(jnp.float32)
            + swapped_cores(blocks[2 * dx + 1]).astype(jnp.float32)
        ).astype(jnp.bfloat16)
        for dx in range(size // 2)
    ]
    arrived = [moved(pairs[dx], dx) for dx in near_first(size)[::-1]]
    return sum(a.astype(jnp.float32) for a in arrived)


def client_place():
    index = lax.axis_index("clients")
    return index // 8, index // 2 % 4


def client_shifted(x, high, y):
    pairs = []
    for i in range(lax.axis_size("clients")):
        pairs.append((i, (i // 8 + high) % 4 * 8 + (i // 2 + y) % 4 * 2 + i % 2))
    return lax.ppermute(x, "clients", pairs)


def collected(block, step, place):
    arrived = [block] + [None] * 3
    for k in range(1, 4):
        arrived[4 - k] = client_shifted(block, k * step[0], k * step[1])
    twice = jnp.stack(arrived + arrived)
    return lax.dynamic_slice_in_dim(twice, (4 - place) % 4, 4)


def reduced(blocks, step, place):
    own = lax.dynamic_index_in_dim(blocks, place, 0, False)
    came = [
        client_shifted(
            lax.dynamic_index_in_dim(blocks, (place + k) % 4, 0, False), k * step[0], k * step[1]
        )
        for k in range(1, 4)
    ]
    return sum(c.astype(jnp.float32) for c in [own] + came)


def turned(x, contract):
    eye = jnp.eye(x.shape[contract], dtype=x.dtype)
    dims = (((1,), (1,)), ((), ())) if contract else (((0,), (0,)), ((), ()))
    both = (eye, x) if contract else (x, eye)
    return lax.dot_general(*both, dims, preferred_element_type=jnp.float32).astype(x.dtype)


def start_gather_clients(x):
    a, rows, cols = x.shape
    return collected(jnp.swapaxes(x, 1, 2).reshape(a * cols, rows), (0, 1), client_place()[1])


def end_gather_clients(mine, a):
    count, wide, rows = mine.shape
    cols = wide // a
    theirs = swapped_cores(mine)
    first = lax.axis_index("clients") % 2 == 0
    both = jnp.stack([jnp.where(first, mine, theirs), jnp.where(first, theirs, mine)], axis=1)
    both = both.reshape(count, 2, a, cols, rows)
    return [both[:, :, k].reshape(count * 2 * cols, rows) for k in range(a)]


def cut_for_clients(array, count):
    rows, cols = array.shape
    return turned(array, 0).reshape(count, 2, cols // (2 * count), rows)


def paired(cuts):
    count, _, part, rows = cuts[0].shape
    cut = jnp.stack(cuts, axis=2).reshape(count, 2, len(cuts) * part, rows)
    core = lax.axis_index("clients") % 2
    kept = lax.dynamic_index_in_dim(cut, core, 1, keepdims=False)
    given = lax.dynamic_index_in_dim(cut, 1 - core, 1, keepdims=False)
    came = swapped_cores(given)
    pair = (kept.astype(jnp.float32) + came.astype(jnp.float32)).astype(jnp.bfloat16)
    return jnp.moveaxis(pair.reshape(4, 4, len(cuts) * part, rows), 1, 0)


GELU_SCALE = math.sqrt(2.0 / math.pi)
GELU_CUBE = 0.044715
TILES = 2


def dot(left, right, left_dim, right_dim):
    dims = (((left_dim,), (right_dim,)), ((), ()))
    return lax.dot_general(left, right, dims, preferred_element_type=jnp.float32)


def step_kernel(size, loss_scale, *refs):
    slabs, (normed, residual), blocks = refs[:size], refs[size : size + 2], refs[size + 2 : -6]
    gate_w, up_w, out_w, hidden, gate_grad, up_grad = refs[-6:]
    rows = slabs[0].shape[0] // 3
    width = rows * size
    for j, slab in enumerate(slabs):
        for k, weights in enumerate((gate_w, up_w, out_w)):
            weights[j * rows : (j + 1) * rows, :] = slab[k * rows : (k + 1) * rows, :]
    tile = normed.shape[0] // TILES
    for t in range(TILES):
        part = pl.ds(t * tile, tile)
        inputs = normed[part, :]
        gate_pre = dot(inputs, gate_w[...], 1, 0)
        up_pre = dot(inputs, up_w[...], 1, 0)
        square = gate_pre * gate_pre
        tanh = jnp.tanh(GELU_SCALE * gate_pre * (1.0 + GELU_CUBE * square))
        half = 0.5 + 0.5 * tanh
        slope = half + gate_pre * (0.5 - 0.5 * tanh * tanh) * (
            GELU_SCALE + (3.0 * GELU_CUBE * GELU_SCALE) * square
        )
        gate_act = gate_pre * half
        hidden_part = (gate_act * up_pre).astype(jnp.bfloat16)
        hidden[part, :] = hidden_part
        projected = dot(hidden_part, out_w[...], 1, 1)
        out_part = ((residual[part, :] + projected) * loss_scale).astype(jnp.bfloat16)
        residual[part, :] = out_part.astype(jnp.float32)
        hidden_grad = dot(out_part, out_w[...], 1, 0)
        gate_grad[part, :] = (hidden_grad * up_pre * slope).astype(jnp.bfloat16)
        up_grad[part, :] = (hidden_grad * gate_act).astype(jnp.bfloat16)
    each = width // 2
    for k, (left, right) in enumerate(((residual, hidden), (normed, gate_grad), (normed, up_grad))):
        k = (k + 2) % 3
        for h in range(2):
            columns = left[:, h * each : (h + 1) * each].astype(jnp.bfloat16)
            term = dot(columns, right[...], 0, 0).astype(jnp.bfloat16)
            for j in range(size // 2):
                blocks[h * (size // 2) + j][k * rows : (k + 1) * rows, :] = term[
                    j * rows : (j + 1) * rows
                ]


def local_terms(normed, residual, slabs, loss_scale):
    size = len(slabs)
    tokens, width = normed.shape
    hidden_size = slabs[0].shape[1]
    vmem = pl.BlockSpec(memory_space=pltpu.VMEM)

    def kernel(*refs):
        ins, outs, (copied, *scratch) = refs[: size + 2], refs[size + 2 : 2 * size + 2], refs[2 * size + 2 :]
        copied[...] = ins[size + 1][...]
        step_kernel(size, loss_scale, *ins[: size + 1], copied, *outs, *scratch)

    return list(
        pl.pallas_call(
            kernel,
            out_shape=[jax.ShapeDtypeStruct(slabs[0].shape, jnp.bfloat16)] * size,
            in_specs=[vmem] * (size + 2),
            out_specs=[vmem] * size,
            scratch_shapes=[pltpu.VMEM((tokens, width), jnp.float32)]
            + [pltpu.VMEM((width, hidden_size), jnp.bfloat16)] * 3
            + [pltpu.VMEM((tokens, hidden_size), jnp.bfloat16)] * 3,
            compiler_params=pltpu.CompilerParams(vmem_limit_bytes=52 * 2**20),
            cost_estimate=pl.CostEstimate(
                flops=12 * tokens * width * hidden_size,
                transcendentals=tokens * hidden_size,
                bytes_accessed=12 * width * hidden_size,
            ),
        )(*slabs, normed, residual)
    )


def body(
    token_ids,
    target,
    embedding,
    norm_gain,
    global_model,
    global_control,
    client_control,
    local_steps,
    client_weight,
):
    size = lax.axis_size("fsdp")
    place = lax.axis_index("fsdp")
    core = lax.axis_index("clients") % 2
    width = embedding.shape[1]
    tok_rows = target.shape[1]
    loss_scale = 1.0 / math.sqrt(tok_rows * size)

    line = start_gather_clients(
        jnp.concatenate([global_model, global_control]).astype(jnp.bfloat16)
    )

    all_ids = lax.all_to_all(
        jnp.broadcast_to(token_ids, (size, tok_rows)), "fsdp", 0, 0, tiled=True
    )
    all_ids, line = lax.optimization_barrier((all_ids, line))
    plane = collected(line, (1, 0), client_place()[0])
    late_target, all_ids = lax.optimization_barrier((target[0], all_ids))
    moved_target = moved(late_target, 0)
    looked_up = embedding.at[all_ids.reshape(-1)].get(mode="promise_in_bounds")
    looked_up, plane, moved_target = lax.optimization_barrier((looked_up, plane, moved_target))
    server = end_gather_clients(plane.reshape(-1, *plane.shape[2:]), 6)
    model_rows = jnp.concatenate([turned(x, 1) for x in server[:3]])
    weights = along_x(model_rows, size)

    worker_place = place - place % 2 + core
    order = jnp.stack([peer(worker_place, j, size) for j in range(size)])
    wanted = (order[:, None] * width + jnp.arange(width)[None, :]).reshape(-1)
    reorder = (jnp.arange(size * width)[:, None] == wanted[None, :]).astype(jnp.bfloat16)
    gain = jnp.dot(
        norm_gain[None], reorder.astype(jnp.float32), precision=lax.Precision.HIGHEST
    )

    x_size = size // 2
    x = place // 2
    arrived = [None] * x_size
    for dx in near_first(size):
        both = lax.dynamic_slice_in_dim(
            looked_up, (x + dx) % x_size * 2 * tok_rows, 2 * tok_rows
        )
        arrived[-dx % x_size] = moved(both, dx)
    arrived, model_rows = lax.optimization_barrier((arrived, model_rows))
    moved_target, weights[0] = lax.optimization_barrier((moved_target, weights[0]))
    goal = jnp.dot(moved_target, reorder, preferred_element_type=jnp.float32)
    goal = lax.optimization_barrier(goal.astype(jnp.bfloat16))
    arrived = jnp.stack(arrived).reshape(x_size, 2, tok_rows, width)
    ours = lax.dynamic_index_in_dim(arrived, core, 1, False)
    theirs = swapped_cores(lax.dynamic_index_in_dim(arrived, 1 - core, 1, False))
    pieces = [p for dx in range(x_size) for p in (ours[dx], theirs[dx])]
    stacked = lax.optimization_barrier(jnp.stack(pieces))
    embedded = jnp.moveaxis(stacked, 0, 1).reshape(tok_rows, size * width)
    widened = embedded.astype(jnp.float32)
    inv_norm = lax.rsqrt(jnp.mean(widened * widened, axis=1, keepdims=True) + norm_eps)
    normed = (widened * inv_norm * gain).astype(jnp.bfloat16)
    residual = widened - goal.astype(jnp.float32)
    slabs = with_other_core(weights)

    control_rows = jnp.concatenate([turned(x, 1) for x in server[3:]])
    client_index = lax.axis_index("clients")
    slots = jnp.arange(local_steps.shape[0])
    step_count = jnp.sum(jnp.where(slots == client_index, local_steps, 0)).astype(jnp.float32)
    own_weight = jnp.sum(jnp.where(slots == client_index, client_weight, 0)).astype(jnp.float32)
    weight_total = jnp.sum(client_weight).astype(jnp.float32)
    second = (step_count > 1.5).astype(jnp.float32)
    own_control = client_control[0].reshape(control_rows.shape)
    correction = control_rows.astype(jnp.float32) - own_control

    grads = summed(local_terms(normed, residual, slabs, loss_scale))
    current = (
        model_rows.astype(jnp.float32) - learning_rate * (grads + correction)
    ).astype(jnp.bfloat16)
    slabs = with_other_core(along_x(current, size))

    count = local_steps.shape[0] // 2
    for_step = (own_weight * (grads + step_count * correction)).astype(jnp.bfloat16)
    for_control = (own_weight / step_count * grads).astype(jnp.bfloat16)
    for_step, for_control, _ = lax.optimization_barrier((for_step, for_control, slabs[0]))
    early = [
        [cut_for_clients(x, count) for x in jnp.split(part, 3)] for part in (for_step, for_control)
    ]
    early = paired([cut for part in early for cut in part])
    normed, early = lax.optimization_barrier((normed, early))
    blocks = local_terms(normed, residual, slabs, loss_scale)
    high, y = client_place()
    early = reduced(early, (0, 1), y)
    blocks, early = lax.optimization_barrier((blocks, early))
    last = second * summed(blocks)
    late = [cut_for_clients(x, count) for x in jnp.split((own_weight * last).astype(jnp.bfloat16), 3)]
    late = reduced(paired(late), (0, 1), y)
    line = (early + jnp.concatenate([late, 0.5 * late], axis=1)).astype(jnp.bfloat16)
    sums = reduced(line, (1, 0), high).reshape(6, -1, line.shape[2])
    sums = jnp.swapaxes(sums, 1, 2)
    update = ((grads + last) / step_count).reshape(client_control.shape)
    steps_total = jnp.sum(local_steps * client_weight).astype(jnp.float32)
    rounded_away = global_control - global_control.astype(jnp.bfloat16).astype(jnp.float32)
    server_step = (sums[:3] + steps_total * rounded_away) / weight_total
    server_control = sums[3:] / weight_total
    return (server_step, server_control, update)


def solution(mesh):
    placed = (
        P("clients", "fsdp"),
        P("clients", "fsdp", None),
        P(None, "fsdp"),
        P(),
        P(None, "fsdp", "clients"),
        P(None, "fsdp", "clients"),
        P("clients", None, "fsdp", None),
        P(),
        P(),
    )
    return jax.shard_map(
        body,
        mesh=mesh,
        in_specs=placed,
        out_specs=(
            P(None, "fsdp", "clients"),
            P(None, "fsdp", "clients"),
            P("clients", None, "fsdp", None),
        ),
        check_vma=False,
    )
```

```python
import math

import jax
import jax.numpy as jnp
from jax import lax
from jax.experimental import pallas as pl
from jax.experimental.pallas import tpu as pltpu
from jax.sharding import PartitionSpec as P

LOCAL = 2


learning_rate = 0.005
norm_eps = 1e-06


BOTH = ("clients", "fsdp")


def moved(block, dx):
    clients, size = lax.axis_size("clients"), lax.axis_size("fsdp")
    pairs = []
    for client in range(clients):
        for place in range(size):
            x = (place // 2 + dx) % (size // 2)
            z, core = place % 2, client % 2
            target = (client - core + z) * size + 2 * x + core
            pairs.append((client * size + place, target))
    return lax.ppermute(block, BOTH, pairs)


def peer(place, offset, size):
    x_size = size // 2
    return ((place // 2 + offset // 2) % x_size) * 2 + ((place % 2) ^ (offset % 2))


def near_first(size):
    x_size = size // 2
    return sorted(range(x_size), key=lambda dx: min(dx, x_size - dx))


def swapped_cores(x):
    return lax.ppermute(x, "clients", [(i, i ^ 1) for i in range(lax.axis_size("clients"))])


def gathered(block, size):
    x_size = size // 2
    arrived = [None] * size
    for dx in near_first(size):
        back = 2 * (-dx % x_size)
        arrived[back] = moved(block, dx)
    for dx in near_first(size):
        back = 2 * (-dx % x_size)
        arrived[back + 1] = swapped_cores(arrived[back])
    return arrived


def summed(blocks, order):
    pairs = [
        (
            blocks[2 * dx].astype(jnp.float32)
            + swapped_cores(blocks[2 * dx + 1]).astype(jnp.float32)
        ).astype(jnp.bfloat16)
        for dx in order
    ]
    arrived = [moved(pair, dx) for pair, dx in zip(pairs, order)]
    return sum(a.astype(jnp.float32) for a in arrived)


def client_place():
    index = lax.axis_index("clients")
    return index // 8, index // 2 % 4


def client_shifted(x, high, y):
    pairs = []
    for i in range(lax.axis_size("clients")):
        pairs.append((i, (i // 8 + high) % 4 * 8 + (i // 2 + y) % 4 * 2 + i % 2))
    return lax.ppermute(x, "clients", pairs)


def collected(block, step, place):
    arrived = [block] + [None] * 3
    for k in range(1, 4):
        arrived[4 - k] = client_shifted(block, k * step[0], k * step[1])
    twice = jnp.stack(arrived + arrived)
    return lax.dynamic_slice_in_dim(twice, (4 - place) % 4, 4)


def reduced(blocks, step, place):
    own = lax.dynamic_index_in_dim(blocks, place, 0, False)
    came = [
        client_shifted(
            lax.dynamic_index_in_dim(blocks, (place + k) % 4, 0, False), k * step[0], k * step[1]
        )
        for k in range(1, 4)
    ]
    return sum(c.astype(jnp.float32) for c in [own] + came)


def turned(x, contract):
    eye = jnp.eye(x.shape[contract], dtype=x.dtype)
    dims = (((1,), (1,)), ((), ())) if contract else (((0,), (0,)), ((), ()))
    both = (eye, x) if contract else (x, eye)
    return lax.dot_general(*both, dims, preferred_element_type=jnp.float32).astype(x.dtype)


def start_gather_clients(x):
    a, rows, cols = x.shape
    return collected(jnp.swapaxes(x, 1, 2).reshape(a * cols, rows), (0, 1), client_place()[1])


def end_gather_clients(mine, a):
    count, wide, rows = mine.shape
    cols = wide // a
    theirs = swapped_cores(mine)
    first = lax.axis_index("clients") % 2 == 0
    both = jnp.stack([jnp.where(first, mine, theirs), jnp.where(first, theirs, mine)], axis=1)
    both = both.reshape(count, 2, a, cols, rows)
    return [both[:, :, k].reshape(count * 2 * cols, rows) for k in range(a)]


def cut_for_clients(array, count):
    rows, cols = array.shape
    return turned(array, 0).reshape(count, 2, cols // (2 * count), rows)


def paired(cuts):
    count, _, part, rows = cuts[0].shape
    cut = jnp.stack(cuts, axis=2).reshape(count, 2, len(cuts) * part, rows)
    core = lax.axis_index("clients") % 2
    kept = lax.dynamic_index_in_dim(cut, core, 1, keepdims=False)
    given = lax.dynamic_index_in_dim(cut, 1 - core, 1, keepdims=False)
    came = swapped_cores(given)
    pair = (kept.astype(jnp.float32) + came.astype(jnp.float32)).astype(jnp.bfloat16)
    return jnp.moveaxis(pair.reshape(4, 4, len(cuts) * part, rows), 1, 0)


GELU_SCALE = math.sqrt(2.0 / math.pi)
GELU_CUBE = 0.044715
TILES = 2


def dot(left, right, left_dim, right_dim):
    dims = (((left_dim,), (right_dim,)), ((), ()))
    return lax.dot_general(left, right, dims, preferred_element_type=jnp.float32)


def step_kernel(size, loss_scale, *refs):
    slabs, (normed, residual), blocks = refs[:size], refs[size : size + 2], refs[size + 2 : -6]
    gate_w, up_w, out_w, hidden, gate_grad, up_grad = refs[-6:]
    rows = slabs[0].shape[0] // 3
    width = rows * size
    for j, slab in enumerate(slabs):
        for k, weights in enumerate((gate_w, up_w, out_w)):
            weights[j * rows : (j + 1) * rows, :] = slab[k * rows : (k + 1) * rows, :]
    tile = normed.shape[0] // TILES
    for t in range(TILES):
        part = pl.ds(t * tile, tile)
        inputs = normed[part, :]
        gate_pre = dot(inputs, gate_w[...], 1, 0)
        up_pre = dot(inputs, up_w[...], 1, 0)
        square = gate_pre * gate_pre
        tanh = jnp.tanh(GELU_SCALE * gate_pre * (1.0 + GELU_CUBE * square))
        half = 0.5 + 0.5 * tanh
        slope = half + gate_pre * (0.5 - 0.5 * tanh * tanh) * (
            GELU_SCALE + (3.0 * GELU_CUBE * GELU_SCALE) * square
        )
        gate_act = gate_pre * half
        hidden_part = (gate_act * up_pre).astype(jnp.bfloat16)
        hidden[part, :] = hidden_part
        projected = dot(hidden_part, out_w[...], 1, 1)
        out_part = ((residual[part, :] + projected) * loss_scale).astype(jnp.bfloat16)
        residual[part, :] = out_part.astype(jnp.float32)
        hidden_grad = dot(out_part, out_w[...], 1, 0)
        gate_grad[part, :] = (hidden_grad * up_pre * slope).astype(jnp.bfloat16)
        up_grad[part, :] = (hidden_grad * gate_act).astype(jnp.bfloat16)
    each = width // 2
    for k, (left, right) in enumerate(((residual, hidden), (normed, gate_grad), (normed, up_grad))):
        k = (k + 2) % 3
        for h in range(2):
            columns = left[:, h * each : (h + 1) * each].astype(jnp.bfloat16)
            term = dot(columns, right[...], 0, 0).astype(jnp.bfloat16)
            for j in range(size // 2):
                blocks[h * (size // 2) + j][k * rows : (k + 1) * rows, :] = term[
                    j * rows : (j + 1) * rows
                ]


def local_terms(normed, residual, slabs, loss_scale):
    size = len(slabs)
    tokens, width = normed.shape
    hidden_size = slabs[0].shape[1]
    vmem = pl.BlockSpec(memory_space=pltpu.VMEM)

    def kernel(*refs):
        ins, outs, (copied, *scratch) = refs[: size + 2], refs[size + 2 : 2 * size + 2], refs[2 * size + 2 :]
        copied[...] = ins[size + 1][...]
        step_kernel(size, loss_scale, *ins[: size + 1], copied, *outs, *scratch)

    return list(
        pl.pallas_call(
            kernel,
            out_shape=[jax.ShapeDtypeStruct(slabs[0].shape, jnp.bfloat16)] * size,
            in_specs=[vmem] * (size + 2),
            out_specs=[vmem] * size,
            scratch_shapes=[pltpu.VMEM((tokens, width), jnp.float32)]
            + [pltpu.VMEM((width, hidden_size), jnp.bfloat16)] * 3
            + [pltpu.VMEM((tokens, hidden_size), jnp.bfloat16)] * 3,
            compiler_params=pltpu.CompilerParams(vmem_limit_bytes=52 * 2**20),
            cost_estimate=pl.CostEstimate(
                flops=12 * tokens * width * hidden_size,
                transcendentals=tokens * hidden_size,
                bytes_accessed=12 * width * hidden_size,
            ),
        )(*slabs, normed, residual)
    )


def body(
    token_ids,
    target,
    embedding,
    norm_gain,
    global_model,
    global_control,
    client_control,
    local_steps,
    client_weight,
):
    size = lax.axis_size("fsdp")
    place = lax.axis_index("fsdp")
    core = lax.axis_index("clients") % 2
    width = embedding.shape[1]
    tok_rows = target.shape[1]
    loss_scale = 1.0 / math.sqrt(tok_rows * size)

    line = start_gather_clients(
        jnp.concatenate([global_model, global_control]).astype(jnp.bfloat16)
    )

    all_ids = lax.all_to_all(
        jnp.broadcast_to(token_ids, (size, tok_rows)), "fsdp", 0, 0, tiled=True
    )
    all_ids, line = lax.optimization_barrier((all_ids, line))
    looked_up = embedding.at[all_ids.reshape(-1)].get(mode="promise_in_bounds")
    plane = collected(line, (1, 0), client_place()[0])
    looked_up, plane = lax.optimization_barrier((looked_up, plane))
    server = end_gather_clients(plane.reshape(-1, *plane.shape[2:]), 6)
    model_rows = jnp.concatenate([turned(x, 1) for x in server[:3]])
    slabs = gathered(model_rows, size)

    worker_place = place - place % 2 + core
    order = jnp.stack([peer(worker_place, j, size) for j in range(size)])
    wanted = (order[:, None] * width + jnp.arange(width)[None, :]).reshape(-1)
    reorder = (jnp.arange(size * width)[:, None] == wanted[None, :]).astype(jnp.bfloat16)
    late_target, looked_up = lax.optimization_barrier((target[0], looked_up))
    goal = jnp.dot(moved(late_target, 0), reorder, preferred_element_type=jnp.float32)
    goal = lax.optimization_barrier(goal.astype(jnp.bfloat16))
    gain = jnp.dot(
        norm_gain[None], reorder.astype(jnp.float32), precision=lax.Precision.HIGHEST
    )

    x_size = size // 2
    x = place // 2
    arrived = [None] * x_size
    for dx in near_first(size):
        both = lax.dynamic_slice_in_dim(
            looked_up, (x + dx) % x_size * 2 * tok_rows, 2 * tok_rows
        )
        arrived[-dx % x_size] = moved(both, dx)
    arrived, model_rows = lax.optimization_barrier((arrived, model_rows))
    arrived = jnp.stack(arrived).reshape(x_size, 2, tok_rows, width)
    ours = lax.dynamic_index_in_dim(arrived, core, 1, False)
    theirs = swapped_cores(lax.dynamic_index_in_dim(arrived, 1 - core, 1, False))
    pieces = [p for dx in range(x_size) for p in (ours[dx], theirs[dx])]
    stacked = lax.optimization_barrier(jnp.stack(pieces))
    embedded = jnp.moveaxis(stacked, 0, 1).reshape(tok_rows, size * width)
    widened = embedded.astype(jnp.float32)
    inv_norm = lax.rsqrt(jnp.mean(widened * widened, axis=1, keepdims=True) + norm_eps)
    normed = (widened * inv_norm * gain).astype(jnp.bfloat16)
    residual = widened - goal.astype(jnp.float32)

    control_rows = jnp.concatenate([turned(x, 1) for x in server[3:]])
    client_index = lax.axis_index("clients")
    slots = jnp.arange(local_steps.shape[0])
    step_count = jnp.sum(jnp.where(slots == client_index, local_steps, 0)).astype(jnp.float32)
    own_weight = jnp.sum(jnp.where(slots == client_index, client_weight, 0)).astype(jnp.float32)
    weight_total = jnp.sum(client_weight).astype(jnp.float32)
    second = (step_count > 1.5).astype(jnp.float32)
    own_control = client_control[0].reshape(control_rows.shape)
    correction = control_rows.astype(jnp.float32) - own_control

    grads = summed(local_terms(normed, residual, slabs, loss_scale), near_first(size))
    current = (
        model_rows.astype(jnp.float32) - learning_rate * (grads + correction)
    ).astype(jnp.bfloat16)
    slabs = gathered(current, size)

    count = local_steps.shape[0] // 2
    for_step = (own_weight * (grads + step_count * correction)).astype(jnp.bfloat16)
    for_control = (own_weight / step_count * grads).astype(jnp.bfloat16)
    for_step, for_control, _ = lax.optimization_barrier((for_step, for_control, slabs[0]))
    early = [
        [cut_for_clients(x, count) for x in jnp.split(part, 3)] for part in (for_step, for_control)
    ]
    early = paired([cut for part in early for cut in part])
    normed, early = lax.optimization_barrier((normed, early))
    blocks = local_terms(normed, residual, slabs, loss_scale)
    high, y = client_place()
    early = reduced(early, (0, 1), y)
    blocks, early = lax.optimization_barrier((blocks, early))
    last = second * summed(blocks, near_first(size)[::-1])
    late = [cut_for_clients(x, count) for x in jnp.split((own_weight * last).astype(jnp.bfloat16), 3)]
    late = reduced(paired(late), (0, 1), y)
    line = (early + jnp.concatenate([late, 0.5 * late], axis=1)).astype(jnp.bfloat16)
    sums = reduced(line, (1, 0), high).reshape(6, -1, line.shape[2])
    sums = jnp.swapaxes(sums, 1, 2)
    update = ((grads + last) / step_count).reshape(client_control.shape)
    steps_total = jnp.sum(local_steps * client_weight).astype(jnp.float32)
    rounded_away = global_control - global_control.astype(jnp.bfloat16).astype(jnp.float32)
    server_step = (sums[:3] + steps_total * rounded_away) / weight_total
    server_control = sums[3:] / weight_total
    return (server_step, server_control, update)


def solution(mesh):
    placed = (
        P("clients", "fsdp"),
        P("clients", "fsdp", None),
        P(None, "fsdp"),
        P(),
        P(None, "fsdp", "clients"),
        P(None, "fsdp", "clients"),
        P("clients", None, "fsdp", None),
        P(),
        P(),
    )
    return jax.shard_map(
        body,
        mesh=mesh,
        in_specs=placed,
        out_specs=(
            P(None, "fsdp", "clients"),
            P(None, "fsdp", "clients"),
            P("clients", None, "fsdp", None),
        ),
        check_vma=False,
    )
```
